256 devices in a mesh: rep: 4 (over x_lo, core), fsdp: 64 (over z, x_hi, y).
Axes of the slice: x: 4 (x_hi: 2, x_lo: 2; x = x_hi * 2 + x_lo), y: 4, z: 8, core: 2. Of those that a mesh axis runs over, the one named last changes fastest.
Arguments:
- tokens: bfloat16 [4096, 4096], P(('rep', 'fsdp')), may hold values from -6 to 6
- readout: bfloat16 [4096, 14336], P('rep', 'fsdp'), may hold values from -0.046875 to 0.046875
- resp_mask: int32 [4096], P('rep'), may hold values 0 or 1
- order: int32 [4, 64], P('rep'), may hold values from 0 to 63, each once within a row
- w_gate: bfloat16 [4, 14336, 4096], P('rep', 'fsdp'), may hold values from -0.09375 to 0.09375
- w_up: bfloat16 [4, 14336, 4096], P('rep', 'fsdp'), may hold values from -0.09375 to 0.09375
- outer_gate: bfloat16 [14336, 4096], P('fsdp', 'rep'), may hold values from -0.09375 to 0.09375
- outer_up: bfloat16 [14336, 4096], P('fsdp', 'rep'), may hold values from -0.09375 to 0.09375
- moment: float32 [14336, 4096], P('fsdp', 'rep'), may hold values from -0.09375 to 0.09375
Outputs:
- loss: float32 [4], P('rep')
- grad_gate: bfloat16 [4, 14336, 4096], P('rep', 'fsdp')
- grad_up: bfloat16 [4, 14336, 4096], P('rep', 'fsdp')
- new_outer: bfloat16 [14336, 4096], P('fsdp', 'rep')
- new_moment: float32 [14336, 4096], P('fsdp', 'rep')
The draws below stay inside these ranges and needn't reach their ends.
Inputs may be any that keep to these rules, and one draw needn't show every extreme that they name: Each row of order holds every sequence number of its group once.
All inputs are finite; a program needn't handle non-finite values. Where the reference program divides by a largest or mean magnitude, that divisor is 1e-20 or more. No bound on the sum of `resp_mask` on one device may be relied on, other than what follows from the above.
Results may differ from the reference program's by a relative error of at most 0.022.
Values may be sent and summed in bfloat16 or wider, within the bound.
A program may use at most 128 MiB of HBM per device.

```python
import jax
import jax.numpy as jnp

D = 4096
FF = 14336
BLOCK = 128
LEN = 16
REPS = 4
GROUP_TOK = 1024
SEQS = 64
PAIRS = 32
TOKENS = 4096


def place_ends(values, rng, low, top_value):
    spot = [jax.random.randint(jax.random.fold_in(rng, axis), (), 0, length) for axis, length in enumerate(values.shape)]
    main_axis = values.shape.index(max(values.shape))
    neighbour = spot[:main_axis] + [(spot[main_axis] + 1) % values.shape[main_axis]] + spot[main_axis + 1:]
    return values.at[tuple(spot)].set(low).at[tuple(neighbour)].set(top_value)


def block_levels(key, dims, split, low, largest):
    level = 1.0
    for dim, blocks in split:
        heights = jax.random.uniform(jax.random.fold_in(jax.random.fold_in(key, 6), dim), (blocks,), jnp.float32, low / len(split), largest / len(split))
        level = level * jnp.repeat(jnp.exp(heights), dims[dim] // blocks).reshape((-1,) + (1,) * (len(dims) - 1 - dim))
    return level


def normal_values(rng, extent, deviation, bound, cuts=(), held_as=jnp.bfloat16):
    result = deviation * jax.random.normal(rng, extent, jnp.float32)
    if cuts:
        result = result * block_levels(rng, extent, cuts, -0.22, 0.18)
    return jnp.clip(result, -bound, bound).astype(held_as)


def setup_inputs(seed: int = 0) -> dict:
    keys = jax.random.split(jax.random.key(seed), 10)
    tokens = normal_values(keys[0], (TOKENS, D), 1.0, 6.0, ((0, 256),))
    readout = normal_values(keys[1], (TOKENS, FF), FF ** -0.5, 0.046875, ((0, 4), (1, 64)))
    resp_mask = place_ends((jax.random.randint(keys[2], (TOKENS,), 0, 4) < 3).astype(jnp.int32), jax.random.fold_in(keys[2], 1), 0, 1)
    order = jax.vmap(lambda own: jax.random.permutation(own, SEQS))(jax.random.split(keys[3], REPS)).reshape((REPS, SEQS)).astype(jnp.int32)
    w_gate = normal_values(keys[4], (REPS, FF, D), D ** -0.5, 0.09375, ((0, 4), (1, 64)))
    w_up = normal_values(keys[5], (REPS, FF, D), D ** -0.5, 0.09375, ((0, 4), (1, 64)))
    outer_gate = normal_values(keys[6], (FF, D), D ** -0.5, 0.09375, ((0, 64), (1, 4)))
    outer_up = normal_values(keys[7], (FF, D), D ** -0.5, 0.09375, ((0, 64), (1, 4)))
    moment = normal_values(keys[8], (FF, D), D ** -0.5, 0.09375, ((0, 64), (1, 4)), jnp.float32)
    return dict(tokens=tokens, readout=readout, resp_mask=resp_mask, order=order, w_gate=w_gate, w_up=w_up, outer_gate=outer_gate, outer_up=outer_up, moment=moment)


dpo_beta = 0.1
outer_rate = 0.7
outer_mu = 0.9
tiny_eps = 1e-6


def swiglu_parts(inputs, gate_w, up_w):
    gate = jnp.dot(inputs, gate_w.T, preferred_element_type=jnp.float32)
    upper = jnp.dot(inputs, up_w.T, preferred_element_type=jnp.float32)
    return gate, upper


def seq_scores(hidden, readout_rows, mask_f):
    per_token = jnp.sum(hidden.astype(jnp.float32) * readout_rows.astype(jnp.float32), axis=1)
    return jnp.sum((per_token * mask_f).reshape(SEQS, LEN), axis=1)


def dequantized(delta):
    blocks = delta.reshape(delta.shape[0], -1, BLOCK)
    scale = (jnp.max(jnp.abs(blocks), axis=2, keepdims=True) + tiny_eps).astype(jnp.bfloat16)
    levels = (blocks / scale.astype(jnp.float32)).astype(jnp.bfloat16)
    return (levels.astype(jnp.float32) * scale.astype(jnp.float32)).reshape(delta.shape)


def reference(tokens, readout, resp_mask, order, w_gate, w_up, outer_gate, outer_up, moment):
    losses = []
    grads_gate = []
    grads_up = []
    total = jnp.zeros(outer_gate.shape, jnp.float32)
    for rep_index in range(REPS):
        lower = rep_index * GROUP_TOK
        inputs = tokens[lower:lower + GROUP_TOK]
        readout_rows = readout[lower:lower + GROUP_TOK]
        mask_f = resp_mask[lower:lower + GROUP_TOK].astype(jnp.float32)
        gate, upper = swiglu_parts(inputs, w_gate[rep_index], w_up[rep_index])
        gate_ref, upper_ref = swiglu_parts(inputs, outer_gate, outer_up)
        hidden = (jax.nn.silu(gate) * upper).astype(jnp.bfloat16)
        hidden_ref = (jax.nn.silu(gate_ref) * upper_ref).astype(jnp.bfloat16)
        score = seq_scores(hidden, readout_rows, mask_f)
        score_ref = seq_scores(hidden_ref, readout_rows, mask_f)
        chosen = order[rep_index, 0::2]
        rejected = order[rep_index, 1::2]
        margin = dpo_beta * ((score[chosen] - score_ref[chosen]) - (score[rejected] - score_ref[rejected]))
        losses.append(jnp.mean(jax.nn.softplus(-margin)))
        weight = dpo_beta * jax.nn.sigmoid(-margin) / PAIRS
        coef = jnp.zeros((SEQS,), jnp.float32).at[chosen].add(-weight).at[rejected].add(weight)
        token_grad = jnp.repeat(coef, LEN) * mask_f
        hidden_grad = token_grad[:, None] * readout_rows.astype(jnp.float32)
        sigma = jax.nn.sigmoid(gate)
        gate_grad = (hidden_grad * upper * sigma * (1.0 + gate * (1.0 - sigma))).astype(jnp.bfloat16)
        up_grad = (hidden_grad * jax.nn.silu(gate)).astype(jnp.bfloat16)
        grads_gate.append(jnp.dot(gate_grad.T, inputs, preferred_element_type=jnp.float32).astype(jnp.bfloat16))
        grads_up.append(jnp.dot(up_grad.T, inputs, preferred_element_type=jnp.float32).astype(jnp.bfloat16))
        delta = outer_gate.astype(jnp.float32) - w_gate[rep_index].astype(jnp.float32)
        total = total + dequantized(delta)
    average = total / REPS
    new_moment = outer_mu * moment + average
    new_outer = (outer_gate.astype(jnp.float32) - outer_rate * (average + outer_mu * new_moment)).astype(jnp.bfloat16)
    return jnp.stack(losses), jnp.stack(grads_gate), jnp.stack(grads_up), new_outer, new_moment
```

```python
import functools
import heapq

import jax
import jax.numpy as jnp
import numpy as np
from jax import lax
from jax.experimental import pallas as pl
from jax.experimental.pallas import tpu as pltpu
from jax.sharding import PartitionSpec as P

BLOCK = 128
LEN = 16
NZ, NX, NY = 8, 2, 4
SEQS = NZ * NX * NY
GROUP_TOK = SEQS * LEN
CHUNK = 256
CHUNKS = GROUP_TOK // CHUNK
PER_CHUNK = CHUNK // LEN

dpo_beta = 0.1
outer_rate = 0.7
outer_mu = 0.9
tiny_eps = 1e-06

MESH = pl.DeviceIdType.MESH
F32 = jnp.float32
BF16 = jnp.bfloat16


def gather_plan():
    arrives = {}
    flip = 0
    for dx in range(NX):
        for dz in range(NZ):
            for dy in range(NY):
                if (dx, dy, dz) == (0, 0, 0):
                    continue
                if dy == 0 and dz == 0:
                    side = "x"
                elif dz != 0 and (dy == 0 or (dx == 0 and dz != 4)):
                    side = "z+" if dz < 4 or (dz == 4 and dx == 0) else "z-"
                elif dy == 2:
                    side = "y+" if flip % 2 == 0 else "y-"
                    flip += 1
                else:
                    side = "y+" if dy == 1 else "y-"
                arrives[(dx, dy, dz)] = side
    return arrives


ARRIVES = gather_plan()


def source(s):
    dx, dy, dz = s
    side = ARRIVES[s]
    if side == "x":
        return (dx ^ 1, dy, dz)
    if side[0] == "y":
        return (dx, (dy + (-1 if side == "y+" else 1)) % NY, dz)
    return (dx, dy, (dz + (-1 if side == "z+" else 1)) % NZ)


def gather_order(wire=2.82, hop=1.7, far=2.5):
    children = {}
    for s in ARRIVES:
        children.setdefault(source(s), []).append(s)

    def depth(s):
        return 1 + max([depth(k) for k in children.get(s, [])], default=0)

    def size(s):
        return 1 + sum(size(k) for k in children.get(s, []))

    sides = ("x", "y+", "y-", "z+", "z-")
    waiting = {side: [] for side in sides}
    busy = {side: False for side in sides}
    events = [(0.0, 0, "arrive", (0, 0, 0))]
    count = 1
    order = []
    while events:
        now, _, kind, what = heapq.heappop(events)
        if kind == "free":
            busy[what] = False
        else:
            order.append(what)
            for k in children.get(what, []):
                waiting[ARRIVES[k]].append(k)
        for side in sides:
            if not busy[side] and waiting[side]:
                waiting[side].sort(key=lambda s: (-depth(s), -size(s)))
                s = waiting[side].pop(0)
                busy[side] = True
                heapq.heappush(events, (now + wire, count, "free", side))
                heapq.heappush(
                    events, (now + wire + (far if side == "x" else hop), count + 1, "arrive", s)
                )
                count += 2
    for kids in children.values():
        kids.sort(key=lambda s: (-depth(s), -size(s)))
    return order, children


ORDER, CHILDREN = gather_order()
RANK = {s: i for i, s in enumerate(ORDER)}


def position_codes():
    codes = np.zeros((1, GROUP_TOK), np.int32)
    for (dx, dy, dz), rank in RANK.items():
        codes[0, rank * LEN:(rank + 1) * LEN] = dz * 8 + dx * 4 + dy
    return codes


def sequence_of(codes):
    me = lax.axis_index("fsdp")
    z, x, y = me // 8, (me // 4) % 2, me % 4
    dz, dx, dy = codes >> 3, (codes >> 2) & 1, codes & 3
    return (((dz + z) & 7) << 3) + (((dx + x) & 1) << 2) + ((dy + y) & 3)


def iota(shape, axis):
    return lax.broadcasted_iota(jnp.int32, shape, axis)


def column_to_row(column, rows, lanes):
    eye = iota((rows, lanes), 0) == iota((rows, lanes), 1)
    return jnp.sum(jnp.where(eye, column, 0.0), axis=0, keepdims=True)


def row_to_column(row, rows, lanes):
    eye = iota((rows, lanes), 0) == iota((rows, lanes), 1)
    return jnp.sum(jnp.where(eye, row, 0.0), axis=1, keepdims=True)


def gather_kernel(
    codes_ref, mask_ref, tokens_hbm, readout_hbm, wg_hbm, wu_hbm, og_hbm, ou_hbm,
    x_out, grads_out, average_out, relative_out,
    x_all, wg, wu, og, ou, own, slabs, readout, grads, average, gate_s, upper_s, token_score,
    near, wide, near_own, wide_own,
    local_sem, send_sem, recv_sem, rep_send, rep_recv, sum_send, sum_recv, out_sem,
):
    units = wg.shape[0]
    width = og.shape[1]
    part = own.shape[1]
    rep = lax.axis_index("rep")
    me = lax.axis_index("fsdp")
    z, x, y = me // 8, (me // 4) % 2, me % 4

    def at(dx, dy, dz):
        return ((z + dz) % 8) * 8 + ((x + dx) % 2) * 4 + (y + dy) % 4

    barrier = pltpu.get_barrier_semaphore()
    peers = [(rep, at(0, 0, d)) for d in range(1, NZ)]
    peers += [(rep, at(d // 4, d % 4, 0)) for d in range(1, NX * NY)]
    peers += [(rep ^ d, me) for d in range(1, 4)]
    for peer in peers:
        pl.semaphore_signal(barrier, inc=1, device_id=peer, device_id_type=MESH)

    def columns(r):
        return pl.ds(pl.multiple_of(r * part, part), part)

    local = [
        pltpu.make_async_copy(tokens_hbm, x_all.at[pl.ds(0, LEN), :], local_sem.at[0]),
        pltpu.make_async_copy(readout_hbm, readout, local_sem.at[1]),
        pltpu.make_async_copy(wg_hbm, wg, local_sem.at[2]),
        pltpu.make_async_copy(wu_hbm, wu, local_sem.at[3]),
        pltpu.make_async_copy(og_hbm, own, local_sem.at[4]),
        pltpu.make_async_copy(og_hbm, og.at[:, columns(rep)], local_sem.at[5]),
        pltpu.make_async_copy(ou_hbm, ou.at[:, columns(rep)], local_sem.at[6]),
        pltpu.make_async_copy(wg_hbm.at[:, columns(rep)], slabs.at[0], local_sem.at[7]),
    ]
    for copy in local:
        copy.start()
    pl.semaphore_wait(barrier, len(peers))

    back = {"x": (1, 0, 0), "y+": (0, -1, 0), "y-": (0, 1, 0), "z+": (0, 0, -1), "z-": (0, 0, 1)}

    def shard_copy(s):
        origin = source(s)
        rank = RANK[s]
        src = tokens_hbm if origin == (0, 0, 0) else x_all.at[pl.ds(RANK[origin] * LEN, LEN), :]
        return pltpu.make_async_remote_copy(
            src_ref=src,
            dst_ref=x_all.at[pl.ds(rank * LEN, LEN), :],
            send_sem=send_sem.at[rank],
            recv_sem=recv_sem.at[rank],
            device_id=(rep, at(*back[ARRIVES[s]])),
            device_id_type=MESH,
        )

    copies = {s: shard_copy(s) for s in ARRIVES}

    def rep_copy(i, src, dst, distance):
        return pltpu.make_async_remote_copy(
            src_ref=src, dst_ref=dst, send_sem=rep_send.at[i], recv_sem=rep_recv.at[i],
            device_id=(rep ^ distance, me), device_id_type=MESH,
        )

    mine, across = columns(rep), columns(rep ^ 2)
    gate_far = rep_copy(0, og_hbm, og.at[:, mine], 2)
    up_far = rep_copy(1, ou_hbm, ou.at[:, mine], 2)
    gate_near = rep_copy(2, og_hbm, og.at[:, mine], 1)
    up_near = rep_copy(3, ou_hbm, ou.at[:, mine], 1)
    gate_pass = rep_copy(4, og.at[:, across], og.at[:, across], 1)
    up_pass = rep_copy(5, ou.at[:, across], ou.at[:, across], 1)
    slab_copies = [
        rep_copy(5 + d, wg_hbm.at[:, columns(rep ^ d)], slabs.at[d], d) for d in (1, 2, 3)
    ]

    for s in CHILDREN[(0, 0, 0)]:
        copies[s].start()
    for copy in (gate_far, gate_near, up_far, up_near, slab_copies[0], slab_copies[1], slab_copies[2]):
        copy.start()

    local[1].wait()
    masked = (readout[...].astype(F32) * mask_ref[...].astype(F32)).astype(BF16)
    sequence = sequence_of(codes_ref[...])
    wanted = sequence * LEN + (iota((1, GROUP_TOK), 1) & (LEN - 1))
    for c in range(CHUNKS):
        lanes = slice(c * CHUNK, (c + 1) * CHUNK)
        pick = (iota((GROUP_TOK, CHUNK), 0) == wanted[:, lanes]).astype(F32).astype(BF16)
        readout[:, lanes] = jnp.dot(masked, pick, preferred_element_type=F32).astype(BF16)
    token_score[...] = jnp.zeros_like(token_score)
    for i in (2, 3):
        local[i].wait()

    def project(weight, c):
        return lax.dot_general(
            weight[...], x_all[pl.ds(c * CHUNK, CHUNK), :], (((1,), (1,)), ((), ())),
            preferred_element_type=F32,
        )

    ROWS = 32

    def unit_gate(weight, c):
        gate_s[...] = project(weight, c)

    def unit_upper(weight, c):
        upper_s[...] = project(weight, c)

    def unit_policy(c):
        lanes = pl.ds(c * CHUNK, CHUNK)

        def body(i, total):
            rows = pl.ds(pl.multiple_of(i * ROWS, ROWS), ROWS)
            gate, upper = gate_s[rows, :], upper_s[rows, :]
            read = readout[rows, lanes].astype(F32)
            sigma = jax.nn.sigmoid(gate)
            silu = gate * sigma
            hidden = (silu * upper).astype(BF16).astype(F32)
            grads[rows, lanes] = read * upper * sigma * (1.0 + gate * (1.0 - sigma))
            grads[pl.ds(pl.multiple_of(units + i * ROWS, ROWS), ROWS), lanes] = read * silu
            return total + jnp.sum(hidden * read, axis=0, keepdims=True)

        total = lax.fori_loop(0, units // ROWS, body, jnp.zeros((1, CHUNK), F32))
        token_score[:, lanes] += total

    def unit_reference(c):
        lanes = pl.ds(c * CHUNK, CHUNK)

        def body(i, total):
            rows = pl.ds(pl.multiple_of(i * ROWS, ROWS), ROWS)
            gate, upper = gate_s[rows, :], upper_s[rows, :]
            read = readout[rows, lanes].astype(F32)
            hidden = (gate * jax.nn.sigmoid(gate) * upper).astype(BF16).astype(F32)
            return total + jnp.sum(hidden * read, axis=0, keepdims=True)

        total = lax.fori_loop(0, units // ROWS, body, jnp.zeros((1, CHUNK), F32))
        token_score[:, lanes] -= total

    def policy_units(c):
        return [
            functools.partial(unit_gate, wg, c),
            functools.partial(unit_upper, wu, c),
            functools.partial(unit_policy, c),
        ]

    def reference_units(c):
        return [
            functools.partial(unit_gate, og, c),
            functools.partial(unit_upper, ou, c),
            functools.partial(unit_reference, c),
        ]

    outs = [
        pltpu.make_async_copy(
            x_all.at[pl.ds(c * CHUNK, CHUNK), :], x_out.at[pl.ds(c * CHUNK, CHUNK), :], out_sem.at[c]
        )
        for c in range(CHUNKS)
    ]

    todo = []
    local[0].wait()
    for rank in range(1, SEQS):
        s = ORDER[rank]
        copies[s].wait_recv()
        for child in CHILDREN.get(s, []):
            copies[child].start()
        if rank == 20:
            gate_far.wait_recv()
            gate_pass.start()
        if rank == 36:
            up_far.wait_recv()
            up_pass.start()
        if rank == 40:
            local[5].wait()
            local[6].wait()
            for copy in (gate_near, up_near, gate_pass, up_pass):
                copy.wait_recv()
            todo += reference_units(0) + reference_units(1)
        if rank % PER_CHUNK == PER_CHUNK - 1:
            c = rank // PER_CHUNK
            outs[c].start()
            todo += policy_units(c)
            if c >= 2:
                todo += reference_units(c)
        if todo:
            todo.pop(0)()
    for unit in todo:
        unit()

    grads_copy = pltpu.make_async_copy(grads, grads_out, out_sem.at[CHUNKS])
    grads_copy.start()

    belongs = iota((SEQS, GROUP_TOK), 0) == sequence
    partial = jnp.sum(jnp.where(belongs, token_score[...], 0.0), axis=1, keepdims=True)
    partial = column_to_row(partial, SEQS, BLOCK)
    near_own[...] = partial
    near_copies = [
        pltpu.make_async_remote_copy(
            src_ref=near_own, dst_ref=near.at[z], send_sem=sum_send.at[d], recv_sem=sum_recv.at[z],
            device_id=(rep, at(0, 0, d)), device_id_type=MESH,
        )
        for d in (4, 3, 5, 2, 6, 1, 7)
    ]
    for copy in near_copies:
        copy.start()
    near[z] = partial

    for copy in slab_copies:
        copy.wait_recv()
    local[4].wait()
    local[7].wait()
    STEP = 16

    def pseudo(i, _):
        rows = pl.ds(pl.multiple_of(i * STEP, STEP), STEP)
        for b in range(part // BLOCK):
            lanes = slice(b * BLOCK, (b + 1) * BLOCK)
            outer = own[rows, lanes].astype(F32)
            total = jnp.zeros((STEP, BLOCK), F32)
            for r in range(4):
                delta = outer - slabs[r, rows, lanes].astype(F32)
                scale = jnp.max(jnp.abs(delta), axis=1, keepdims=True) + tiny_eps
                scale = scale.astype(BF16).astype(F32)
                total += (delta / scale).astype(BF16).astype(F32) * scale
            average[rows, lanes] = total * 0.25
        return 0

    half = units // STEP // 2
    lax.fori_loop(0, half, pseudo, 0)

    for d in range(1, NZ):
        pltpu.make_async_remote_copy(
            src_ref=near_own, dst_ref=near.at[(z + d) % 8], send_sem=sum_send.at[d],
            recv_sem=sum_recv.at[(z + d) % 8], device_id=(rep, at(0, 0, d)), device_id_type=MESH,
        ).wait_recv()
    partial = near[0]
    for i in range(1, NZ):
        partial = partial + near[i]
    plane = x * 4 + y
    wide_own[...] = partial
    wide_copies = [
        pltpu.make_async_remote_copy(
            src_ref=wide_own, dst_ref=wide.at[plane], send_sem=sum_send.at[8 + d],
            recv_sem=sum_recv.at[8 + plane], device_id=(rep, at(d // 4, d % 4, 0)), device_id_type=MESH,
        )
        for d in (6, 5, 7, 2, 4, 1, 3)
    ]
    for copy in wide_copies:
        copy.start()
    wide[plane] = partial

    lax.fori_loop(half, units // STEP, pseudo, 0)
    average_copy = pltpu.make_async_copy(average, average_out, out_sem.at[CHUNKS + 1])
    average_copy.start()

    for d in range(1, NX * NY):
        other = ((x + d // 4) % 2) * 4 + (y + d % 4) % 4
        pltpu.make_async_remote_copy(
            src_ref=wide_own, dst_ref=wide.at[other], send_sem=sum_send.at[8 + d],
            recv_sem=sum_recv.at[8 + other], device_id=(rep, at(d // 4, d % 4, 0)), device_id_type=MESH,
        ).wait_recv()
    partial = wide[0]
    for i in range(1, NX * NY):
        partial = partial + wide[i]
    relative_out[...] = partial

    for s in ORDER[1:]:
        copies[s].wait_send()
    for copy in (gate_far, up_far, gate_near, up_near, gate_pass, up_pass, *slab_copies):
        copy.wait_send()
    for copy in near_copies + wide_copies:
        copy.wait_send()
    for copy in outs:
        copy.wait()
    grads_copy.wait()
    average_copy.wait()


def gather_forward(codes, mask, tokens, readout_t, w_gate, w_up, outer_gate, outer_up):
    units, width = w_gate.shape
    part = outer_gate.shape[1]
    any_spec = pl.BlockSpec(memory_space=pl.ANY)
    vmem_spec = pl.BlockSpec(memory_space=pltpu.VMEM)
    return pl.pallas_call(
        gather_kernel,
        name="gather_forward",
        out_shape=(
            jax.ShapeDtypeStruct((GROUP_TOK, width), BF16),
            jax.ShapeDtypeStruct((2 * units, GROUP_TOK), F32),
            jax.ShapeDtypeStruct((units, part), F32),
            jax.ShapeDtypeStruct((1, BLOCK), F32),
        ),
        in_specs=[vmem_spec] * 2 + [any_spec] * 6,
        out_specs=(any_spec, any_spec, any_spec, vmem_spec),
        scratch_shapes=[
            pltpu.VMEM((GROUP_TOK, width), BF16),
            pltpu.VMEM((units, width), BF16),
            pltpu.VMEM((units, width), BF16),
            pltpu.VMEM((units, width), BF16),
            pltpu.VMEM((units, width), BF16),
            pltpu.VMEM((units, part), BF16),
            pltpu.VMEM((4, units, part), BF16),
            pltpu.VMEM((units, GROUP_TOK), BF16),
            pltpu.VMEM((2 * units, GROUP_TOK), F32),
            pltpu.VMEM((units, part), F32),
            pltpu.VMEM((units, CHUNK), F32),
            pltpu.VMEM((units, CHUNK), F32),
            pltpu.VMEM((1, GROUP_TOK), F32),
            pltpu.VMEM((NZ, 1, BLOCK), F32),
            pltpu.VMEM((NX * NY, 1, BLOCK), F32),
            pltpu.VMEM((1, BLOCK), F32),
            pltpu.VMEM((1, BLOCK), F32),
            pltpu.SemaphoreType.DMA((8,)),
            pltpu.SemaphoreType.DMA((SEQS,)),
            pltpu.SemaphoreType.DMA((SEQS,)),
            pltpu.SemaphoreType.DMA((9,)),
            pltpu.SemaphoreType.DMA((9,)),
            pltpu.SemaphoreType.DMA((16,)),
            pltpu.SemaphoreType.DMA((16,)),
            pltpu.SemaphoreType.DMA((CHUNKS + 2,)),
        ],
        compiler_params=pltpu.CompilerParams(collective_id=0, has_side_effects=True),
    )(codes, mask, tokens, readout_t, w_gate, w_up, outer_gate, outer_up)


def backward_kernel(
    codes_ref, order_ref, relative_ref, grads_ref, x_ref, average_ref, outer_ref, moment_ref,
    loss_out, gate_out, up_out, outer_out, moment_out,
    rows_s,
):
    units = gate_out.shape[1]
    pairs = SEQS // 2

    @pl.when(pl.program_id(0) == 0)
    def _():
        relative = row_to_column(relative_ref[...], SEQS, BLOCK)
        placed = iota((SEQS, SEQS), 0) == order_ref[...]
        by_place = jnp.sum(jnp.where(placed, relative, 0.0), axis=0, keepdims=True)
        place, pair = iota((pairs, SEQS), 1), iota((pairs, SEQS), 0)
        chosen, rejected = place == 2 * pair, place == 2 * pair + 1
        sign = jnp.where(chosen, 1.0, jnp.where(rejected, -1.0, 0.0))
        margin = dpo_beta * jnp.sum(sign * by_place, axis=1, keepdims=True)
        loss_out[0] = jnp.sum(jax.nn.softplus(-margin)) / pairs
        weight = dpo_beta * jax.nn.sigmoid(-margin) / pairs
        place_coef = jnp.sum(-sign * weight, axis=0, keepdims=True)
        coef = jnp.sum(jnp.where(placed, place_coef, 0.0), axis=1, keepdims=True)
        belongs = iota((SEQS, GROUP_TOK), 0) == sequence_of(codes_ref[...])
        token_grad = jnp.sum(jnp.where(belongs, coef, 0.0), axis=0, keepdims=True)
        rows_s[...] = (grads_ref[...] * token_grad).astype(BF16)

    out = jnp.dot(rows_s[...], x_ref[...], preferred_element_type=F32).astype(BF16)
    gate_out[0] = out[:units]
    up_out[0] = out[units:]
    average = average_ref[...]
    new_moment = outer_mu * moment_ref[...] + average
    moment_out[...] = new_moment
    outer_out[...] = (
        outer_ref[...].astype(F32) - outer_rate * (average + outer_mu * new_moment)
    ).astype(BF16)


def backward(codes, order, relative, grads, x_all, average, outer_gate, moment):
    units, part = outer_gate.shape
    width = x_all.shape[1]
    steps = 8
    block, slab = width // steps, part // steps
    whole = lambda i: (0, 0)
    column = lambda i: (0, i)
    once = pl.Buffered(1)
    return pl.pallas_call(
        backward_kernel,
        name="backward",
        grid=(steps,),
        out_shape=(
            jax.ShapeDtypeStruct((1,), F32),
            jax.ShapeDtypeStruct((1, units, width), BF16),
            jax.ShapeDtypeStruct((1, units, width), BF16),
            jax.ShapeDtypeStruct((units, part), BF16),
            jax.ShapeDtypeStruct((units, part), F32),
        ),
        in_specs=[
            pl.BlockSpec(codes.shape, whole),
            pl.BlockSpec(order.shape, whole),
            pl.BlockSpec(relative.shape, whole),
            pl.BlockSpec(grads.shape, whole, pipeline_mode=once),
            pl.BlockSpec((GROUP_TOK, block), column),
            pl.BlockSpec((units, slab), column),
            pl.BlockSpec((units, slab), column),
            pl.BlockSpec((units, slab), column),
        ],
        out_specs=(
            pl.BlockSpec(memory_space=pltpu.SMEM),
            pl.BlockSpec((1, units, block), lambda i: (0, 0, i)),
            pl.BlockSpec((1, units, block), lambda i: (0, 0, i)),
            pl.BlockSpec((units, slab), column),
            pl.BlockSpec((units, slab), column),
        ),
        scratch_shapes=[pltpu.VMEM((2 * units, GROUP_TOK), BF16)],
        compiler_params=pltpu.CompilerParams(dimension_semantics=("arbitrary",)),
    )(codes, order, relative, grads, x_all, average, outer_gate, moment)


def per_device(tokens, readout, resp_mask, order, w_gate, w_up, outer_gate, outer_up, moment):
    codes = jnp.asarray(position_codes())
    x_all, grads, average, relative = gather_forward(
        codes, resp_mask.reshape(1, -1), tokens, readout.T, w_gate[0], w_up[0], outer_gate, outer_up
    )
    return backward(codes, order, relative, grads, x_all, average, outer_gate, moment)


def solution(mesh):
    return jax.shard_map(
        per_device,
        mesh=mesh,
        in_specs=(
            P(("rep", "fsdp"), None),
            P("rep", "fsdp"),
            P("rep"),
            P("rep", None),
            P("rep", "fsdp", None),
            P("rep", "fsdp", None),
            P("fsdp", "rep"),
            P("fsdp", "rep"),
            P("fsdp", "rep"),
        ),
        out_specs=(
            P("rep"),
            P("rep", "fsdp", None),
            P("rep", "fsdp", None),
            P("fsdp", "rep"),
            P("fsdp", "rep"),
        ),
        check_vma=False,
    )
```

```python
import functools
import heapq

import jax
import jax.numpy as jnp
import numpy as np
from jax import lax
from jax.experimental import pallas as pl
from jax.experimental.pallas import tpu as pltpu
from jax.sharding import PartitionSpec as P

BLOCK = 128
LEN = 16
NZ, NX, NY = 8, 2, 4
SEQS = NZ * NX * NY
GROUP_TOK = SEQS * LEN
CHUNK = 256
CHUNKS = GROUP_TOK // CHUNK
PER_CHUNK = CHUNK // LEN
PIECES = 2

dpo_beta = 0.1
outer_rate = 0.7
outer_mu = 0.9
tiny_eps = 1e-06

MESH = pl.DeviceIdType.MESH
F32 = jnp.float32
BF16 = jnp.bfloat16


def gather_plan():
    arrives = {}
    flip = 0
    for dx in range(NX):
        for dz in range(NZ):
            for dy in range(NY):
                if (dx, dy, dz) == (0, 0, 0):
                    continue
                if dy == 0 and dz == 0:
                    side = "x"
                elif dz != 0 and (dy == 0 or (dx == 1 and dz != 4)):
                    side = "z+" if dz < 4 or (dz == 4 and dx == 0) else "z-"
                elif dy == 2:
                    side = "y+" if flip % 2 == 0 else "y-"
                    flip += 1
                else:
                    side = "y+" if dy == 1 else "y-"
                arrives[(dx, dy, dz)] = side
    return arrives


ARRIVES = gather_plan()


def source(s):
    dx, dy, dz = s
    side = ARRIVES[s]
    if side == "x":
        return (dx ^ 1, dy, dz)
    if side[0] == "y":
        return (dx, (dy + (-1 if side == "y+" else 1)) % NY, dz)
    return (dx, dy, (dz + (-1 if side == "z+" else 1)) % NZ)


def gather_order(wire=2.73 / PIECES, hop=2.2, far=3.0):
    children = {}
    for s in ARRIVES:
        children.setdefault(source(s), []).append(s)

    def depth(s):
        return 1 + max([depth(k) for k in children.get(s, [])], default=0)

    for kids in children.values():
        kids.sort(key=lambda s: -depth(s))
    free = {side: 0.0 for side in ("x", "y+", "y-", "z+", "z-")}
    events = [(0.0, p, (0, 0, 0), p) for p in range(PIECES)]
    count = PIECES
    order = []
    while events:
        now, _, s, p = heapq.heappop(events)
        order.append((s, p))
        for kid in children.get(s, []):
            side = ARRIVES[kid]
            free[side] = max(free[side], now) + wire
            heapq.heappush(events, (free[side] + (far if side == "x" else hop), count, kid, p))
            count += 1
    return order, children


ORDER, CHILDREN = gather_order()
RANK = {}
for _s, _p in ORDER:
    if _p == PIECES - 1:
        RANK[_s] = len(RANK)


def position_codes():
    codes = np.zeros((1, GROUP_TOK), np.int32)
    for (dx, dy, dz), rank in RANK.items():
        codes[0, rank * LEN:(rank + 1) * LEN] = dz * 8 + dx * 4 + dy
    return codes


def sequence_of(codes):
    me = lax.axis_index("fsdp")
    z, x, y = me // 8, (me // 4) % 2, me % 4
    dz, dx, dy = codes >> 3, (codes >> 2) & 1, codes & 3
    return (((dz + z) & 7) << 3) + (((dx + x) & 1) << 2) + ((dy + y) & 3)


def iota(shape, axis):
    return lax.broadcasted_iota(jnp.int32, shape, axis)


def column_to_row(column, rows, lanes):
    eye = iota((rows, lanes), 0) == iota((rows, lanes), 1)
    return jnp.sum(jnp.where(eye, column, 0.0), axis=0, keepdims=True)


def row_to_column(row, rows, lanes):
    eye = iota((rows, lanes), 0) == iota((rows, lanes), 1)
    return jnp.sum(jnp.where(eye, row, 0.0), axis=1, keepdims=True)


def gather_kernel(
    codes_ref, mask_ref, tokens_hbm, readout_hbm, wg_hbm, wu_hbm, og_hbm, ou_hbm,
    x_out, grads_out, average_out, relative_out,
    x_all, wg, wu, og, ou, own, slabs, readout, grads, average, gate_s, upper_s, token_score,
    near, wide, near_own, wide_own,
    local_sem, send_sem, recv_sem, rep_send, rep_recv, sum_send, sum_recv, out_sem,
):
    units = wg.shape[0]
    width = wg.shape[1]
    part = own.shape[1]
    rep = lax.axis_index("rep")
    me = lax.axis_index("fsdp")
    z, x, y = me // 8, (me // 4) % 2, me % 4

    def at(dx, dy, dz):
        return ((z + dz) % 8) * 8 + ((x + dx) % 2) * 4 + (y + dy) % 4

    barrier = pltpu.get_barrier_semaphore()
    peers = [(rep, at(0, 0, d)) for d in range(1, NZ)]
    peers += [(rep, at(d // 4, d % 4, 0)) for d in range(1, NX * NY)]
    peers += [(rep ^ d, me) for d in range(1, 4)]
    for peer in peers:
        pl.semaphore_signal(barrier, inc=1, device_id=peer, device_id_type=MESH)

    def columns(r):
        return pl.ds(pl.multiple_of(r * part, part), part)

    local = [
        pltpu.make_async_copy(tokens_hbm, x_all.at[pl.ds(0, LEN), :], local_sem.at[0]),
        pltpu.make_async_copy(readout_hbm, readout, local_sem.at[1]),
        pltpu.make_async_copy(wg_hbm, wg, local_sem.at[2]),
        pltpu.make_async_copy(wu_hbm, wu, local_sem.at[3]),
        pltpu.make_async_copy(og_hbm, own, local_sem.at[4]),
        pltpu.make_async_copy(og_hbm, og.at[:, columns(rep)], local_sem.at[5]),
        pltpu.make_async_copy(ou_hbm, ou.at[:, columns(rep)], local_sem.at[6]),
        pltpu.make_async_copy(wg_hbm.at[:, columns(rep)], slabs.at[0], local_sem.at[7]),
    ]
    for copy in local:
        copy.start()
    pl.semaphore_wait(barrier, len(peers))

    back = {"x": (1, 0, 0), "y+": (0, -1, 0), "y-": (0, 1, 0), "z+": (0, 0, -1), "z-": (0, 0, 1)}

    def piece_copy(s, p):
        origin = source(s)
        rank = RANK[s]
        lanes = pl.ds(p * (width // PIECES), width // PIECES)
        if origin == (0, 0, 0):
            src = tokens_hbm.at[:, lanes]
        else:
            src = x_all.at[pl.ds(RANK[origin] * LEN, LEN), lanes]
        return pltpu.make_async_remote_copy(
            src_ref=src,
            dst_ref=x_all.at[pl.ds(rank * LEN, LEN), lanes],
            send_sem=send_sem.at[rank * PIECES + p],
            recv_sem=recv_sem.at[rank * PIECES + p],
            device_id=(rep, at(*back[ARRIVES[s]])),
            device_id_type=MESH,
        )

    copies = {(s, p): piece_copy(s, p) for s in ARRIVES for p in range(PIECES)}

    def rep_copy(i, src, dst, distance):
        return pltpu.make_async_remote_copy(
            src_ref=src, dst_ref=dst, send_sem=rep_send.at[i], recv_sem=rep_recv.at[i],
            device_id=(rep ^ distance, me), device_id_type=MESH,
        )

    mine, across = columns(rep), columns(rep ^ 2)
    gate_far = rep_copy(0, og_hbm, og.at[:, mine], 2)
    up_far = rep_copy(1, ou_hbm, ou.at[:, mine], 2)
    gate_near = rep_copy(2, og_hbm, og.at[:, mine], 1)
    up_near = rep_copy(3, ou_hbm, ou.at[:, mine], 1)
    gate_pass = rep_copy(4, og.at[:, across], og.at[:, across], 1)
    up_pass = rep_copy(5, ou.at[:, across], ou.at[:, across], 1)
    slab_copies = [
        rep_copy(5 + d, wg_hbm.at[:, columns(rep ^ d)], slabs.at[d], d) for d in (1, 2, 3)
    ]

    for p in range(PIECES):
        for s in CHILDREN[(0, 0, 0)]:
            copies[s, p].start()
    for copy in (gate_far, gate_near, up_far, up_near, slab_copies[0], slab_copies[1], slab_copies[2]):
        copy.start()

    local[1].wait()
    masked = (readout[...].astype(F32) * mask_ref[...].astype(F32)).astype(BF16)
    sequence = sequence_of(codes_ref[...])
    wanted = sequence * LEN + (iota((1, GROUP_TOK), 1) & (LEN - 1))
    for c in range(CHUNKS):
        lanes = slice(c * CHUNK, (c + 1) * CHUNK)
        pick = (iota((GROUP_TOK, CHUNK), 0) == wanted[:, lanes]).astype(F32).astype(BF16)
        readout[:, lanes] = jnp.dot(masked, pick, preferred_element_type=F32).astype(BF16)
    token_score[...] = jnp.zeros_like(token_score)
    for i in (2, 3):
        local[i].wait()

    def project(weight, c):
        return lax.dot_general(
            weight[...], x_all[pl.ds(c * CHUNK, CHUNK), :], (((1,), (1,)), ((), ())),
            preferred_element_type=F32,
        )

    ROWS = 32

    def unit_gate(weight, c):
        gate_s[...] = project(weight, c)

    def unit_upper(weight, c):
        upper_s[...] = project(weight, c)

    def unit_policy(c):
        lanes = pl.ds(c * CHUNK, CHUNK)

        def body(i, total):
            rows = pl.ds(pl.multiple_of(i * ROWS, ROWS), ROWS)
            gate, upper = gate_s[rows, :], upper_s[rows, :]
            read = readout[rows, lanes].astype(F32)
            sigma = jax.nn.sigmoid(gate)
            silu = gate * sigma
            hidden = (silu * upper).astype(BF16).astype(F32)
            grads[rows, lanes] = read * upper * sigma * (1.0 + gate * (1.0 - sigma))
            grads[pl.ds(pl.multiple_of(units + i * ROWS, ROWS), ROWS), lanes] = read * silu
            return total + jnp.sum(hidden * read, axis=0, keepdims=True)

        total = lax.fori_loop(0, units // ROWS, body, jnp.zeros((1, CHUNK), F32))
        token_score[:, lanes] += total

    def unit_reference(c):
        lanes = pl.ds(c * CHUNK, CHUNK)

        def body(i, total):
            rows = pl.ds(pl.multiple_of(i * ROWS, ROWS), ROWS)
            gate, upper = gate_s[rows, :], upper_s[rows, :]
            read = readout[rows, lanes].astype(F32)
            hidden = (gate * jax.nn.sigmoid(gate) * upper).astype(BF16).astype(F32)
            return total + jnp.sum(hidden * read, axis=0, keepdims=True)

        total = lax.fori_loop(0, units // ROWS, body, jnp.zeros((1, CHUNK), F32))
        token_score[:, lanes] -= total

    def policy_units(c):
        return [
            functools.partial(unit_gate, wg, c),
            functools.partial(unit_upper, wu, c),
            functools.partial(unit_policy, c),
        ]

    def reference_units(c):
        return [
            functools.partial(unit_gate, og, c),
            functools.partial(unit_upper, ou, c),
            functools.partial(unit_reference, c),
        ]

    outs = [
        pltpu.make_async_copy(
            x_all.at[pl.ds(c * CHUNK, CHUNK), :], x_out.at[pl.ds(c * CHUNK, CHUNK), :], out_sem.at[c]
        )
        for c in range(CHUNKS)
    ]

    todo = []
    local[0].wait()
    for s, p in ORDER[PIECES:]:
        copies[s, p].wait_recv()
        for child in CHILDREN.get(s, []):
            copies[child, p].start()
        if p < PIECES - 1:
            continue
        rank = RANK[s]
        if rank == 20:
            gate_far.wait_recv()
            gate_pass.start()
        if rank == 36:
            up_far.wait_recv()
            up_pass.start()
        if rank == 40:
            local[5].wait()
            local[6].wait()
            for copy in (gate_near, up_near, gate_pass, up_pass):
                copy.wait_recv()
            todo += reference_units(0) + reference_units(1)
        if rank % PER_CHUNK == PER_CHUNK - 1:
            c = rank // PER_CHUNK
            outs[c].start()
            todo += policy_units(c)
            if c >= 2:
                todo += reference_units(c)
        if todo:
            todo.pop(0)()
    for unit in todo:
        unit()

    grads_copy = pltpu.make_async_copy(grads, grads_out, out_sem.at[CHUNKS])
    grads_copy.start()

    belongs = iota((SEQS, GROUP_TOK), 0) == sequence
    partial = jnp.sum(jnp.where(belongs, token_score[...], 0.0), axis=1, keepdims=True)
    partial = column_to_row(partial, SEQS, BLOCK)
    near_own[...] = partial
    near_copies = [
        pltpu.make_async_remote_copy(
            src_ref=near_own, dst_ref=near.at[z], send_sem=sum_send.at[d], recv_sem=sum_recv.at[z],
            device_id=(rep, at(0, 0, d)), device_id_type=MESH,
        )
        for d in (4, 3, 5, 2, 6, 1, 7)
    ]
    for copy in near_copies:
        copy.start()
    near[z] = partial

    for copy in slab_copies:
        copy.wait_recv()
    local[4].wait()
    local[7].wait()
    STEP = 16

    def pseudo(i, _):
        rows = pl.ds(pl.multiple_of(i * STEP, STEP), STEP)
        for b in range(part // BLOCK):
            lanes = slice(b * BLOCK, (b + 1) * BLOCK)
            outer = own[rows, lanes].astype(F32)
            total = jnp.zeros((STEP, BLOCK), F32)
            for r in range(4):
                delta = outer - slabs[r, rows, lanes].astype(F32)
                scale = jnp.max(jnp.abs(delta), axis=1, keepdims=True) + tiny_eps
                scale = scale.astype(BF16).astype(F32)
                total += (delta / scale).astype(BF16).astype(F32) * scale
            average[rows, lanes] = total * 0.25
        return 0

    half = units // STEP // 2
    lax.fori_loop(0, half, pseudo, 0)

    for d in range(1, NZ):
        pltpu.make_async_remote_copy(
            src_ref=near_own, dst_ref=near.at[(z + d) % 8], send_sem=sum_send.at[d],
            recv_sem=sum_recv.at[(z + d) % 8], device_id=(rep, at(0, 0, d)), device_id_type=MESH,
        ).wait_recv()
    partial = near[0]
    for i in range(1, NZ):
        partial = partial + near[i]
    plane = x * 4 + y
    wide_own[...] = partial
    wide_copies = [
        pltpu.make_async_remote_copy(
            src_ref=wide_own, dst_ref=wide.at[plane], send_sem=sum_send.at[8 + d],
            recv_sem=sum_recv.at[8 + plane], device_id=(rep, at(d // 4, d % 4, 0)), device_id_type=MESH,
        )
        for d in (6, 5, 7, 2, 4, 1, 3)
    ]
    for copy in wide_copies:
        copy.start()
    wide[plane] = partial

    lax.fori_loop(half, units // STEP, pseudo, 0)
    average_copy = pltpu.make_async_copy(average, average_out, out_sem.at[CHUNKS + 1])
    average_copy.start()

    for d in range(1, NX * NY):
        other = ((x + d // 4) % 2) * 4 + (y + d % 4) % 4
        pltpu.make_async_remote_copy(
            src_ref=wide_own, dst_ref=wide.at[other], send_sem=sum_send.at[8 + d],
            recv_sem=sum_recv.at[8 + other], device_id=(rep, at(d // 4, d % 4, 0)), device_id_type=MESH,
        ).wait_recv()
    partial = wide[0]
    for i in range(1, NX * NY):
        partial = partial + wide[i]
    relative_out[...] = partial

    for piece in ORDER[PIECES:]:
        copies[piece].wait_send()
    for copy in (gate_far, up_far, gate_near, up_near, gate_pass, up_pass, *slab_copies):
        copy.wait_send()
    for copy in near_copies + wide_copies:
        copy.wait_send()
    for copy in outs:
        copy.wait()
    grads_copy.wait()
    average_copy.wait()


def gather_forward(codes, mask, tokens, readout_t, w_gate, w_up, outer_gate, outer_up):
    units, width = w_gate.shape
    part = outer_gate.shape[1]
    any_spec = pl.BlockSpec(memory_space=pl.ANY)
    vmem_spec = pl.BlockSpec(memory_space=pltpu.VMEM)
    return pl.pallas_call(
        gather_kernel,
        name="gather_forward",
        out_shape=(
            jax.ShapeDtypeStruct((GROUP_TOK, width), BF16),
            jax.ShapeDtypeStruct((2 * units, GROUP_TOK), F32),
            jax.ShapeDtypeStruct((units, part), F32),
            jax.ShapeDtypeStruct((1, BLOCK), F32),
        ),
        in_specs=[vmem_spec] * 2 + [any_spec] * 6,
        out_specs=(any_spec, any_spec, any_spec, vmem_spec),
        scratch_shapes=[
            pltpu.VMEM((GROUP_TOK, width), BF16),
            pltpu.VMEM((units, width), BF16),
            pltpu.VMEM((units, width), BF16),
            pltpu.VMEM((units, width), BF16),
            pltpu.VMEM((units, width), BF16),
            pltpu.VMEM((units, part), BF16),
            pltpu.VMEM((4, units, part), BF16),
            pltpu.VMEM((units, GROUP_TOK), BF16),
            pltpu.VMEM((2 * units, GROUP_TOK), F32),
            pltpu.VMEM((units, part), F32),
            pltpu.VMEM((units, CHUNK), F32),
            pltpu.VMEM((units, CHUNK), F32),
            pltpu.VMEM((1, GROUP_TOK), F32),
            pltpu.VMEM((NZ, 1, BLOCK), F32),
            pltpu.VMEM((NX * NY, 1, BLOCK), F32),
            pltpu.VMEM((1, BLOCK), F32),
            pltpu.VMEM((1, BLOCK), F32),
            pltpu.SemaphoreType.DMA((8,)),
            pltpu.SemaphoreType.DMA((SEQS * PIECES,)),
            pltpu.SemaphoreType.DMA((SEQS * PIECES,)),
            pltpu.SemaphoreType.DMA((9,)),
            pltpu.SemaphoreType.DMA((9,)),
            pltpu.SemaphoreType.DMA((16,)),
            pltpu.SemaphoreType.DMA((16,)),
            pltpu.SemaphoreType.DMA((CHUNKS + 2,)),
        ],
        compiler_params=pltpu.CompilerParams(collective_id=0, has_side_effects=True),
    )(codes, mask, tokens, readout_t, w_gate, w_up, outer_gate, outer_up)


def backward_kernel(
    codes_ref, order_ref, relative_ref, grads_ref, x_ref, average_ref, outer_ref, moment_ref,
    loss_out, gate_out, up_out, outer_out, moment_out,
    rows_s,
):
    units = gate_out.shape[1]
    pairs = SEQS // 2

    @pl.when(pl.program_id(0) == 0)
    def _():
        relative = row_to_column(relative_ref[...], SEQS, BLOCK)
        placed = iota((SEQS, SEQS), 0) == order_ref[...]
        by_place = jnp.sum(jnp.where(placed, relative, 0.0), axis=0, keepdims=True)
        place, pair = iota((pairs, SEQS), 1), iota((pairs, SEQS), 0)
        chosen, rejected = place == 2 * pair, place == 2 * pair + 1
        sign = jnp.where(chosen, 1.0, jnp.where(rejected, -1.0, 0.0))
        margin = dpo_beta * jnp.sum(sign * by_place, axis=1, keepdims=True)
        loss_out[0] = jnp.sum(jax.nn.softplus(-margin)) / pairs
        weight = dpo_beta * jax.nn.sigmoid(-margin) / pairs
        place_coef = jnp.sum(-sign * weight, axis=0, keepdims=True)
        coef = jnp.sum(jnp.where(placed, place_coef, 0.0), axis=1, keepdims=True)
        belongs = iota((SEQS, GROUP_TOK), 0) == sequence_of(codes_ref[...])
        token_grad = jnp.sum(jnp.where(belongs, coef, 0.0), axis=0, keepdims=True)
        rows_s[...] = (grads_ref[...] * token_grad).astype(BF16)

    out = jnp.dot(rows_s[...], x_ref[...], preferred_element_type=F32).astype(BF16)
    gate_out[0] = out[:units]
    up_out[0] = out[units:]
    average = average_ref[...]
    new_moment = outer_mu * moment_ref[...] + average
    moment_out[...] = new_moment
    outer_out[...] = (
        outer_ref[...].astype(F32) - outer_rate * (average + outer_mu * new_moment)
    ).astype(BF16)


def backward(codes, order, relative, grads, x_all, average, outer_gate, moment):
    units, part = outer_gate.shape
    width = x_all.shape[1]
    steps = 8
    block, slab = width // steps, part // steps
    whole = lambda i: (0, 0)
    column = lambda i: (0, i)
    once = pl.Buffered(1)
    return pl.pallas_call(
        backward_kernel,
        name="backward",
        grid=(steps,),
        out_shape=(
            jax.ShapeDtypeStruct((1,), F32),
            jax.ShapeDtypeStruct((1, units, width), BF16),
            jax.ShapeDtypeStruct((1, units, width), BF16),
            jax.ShapeDtypeStruct((units, part), BF16),
            jax.ShapeDtypeStruct((units, part), F32),
        ),
        in_specs=[
            pl.BlockSpec(codes.shape, whole),
            pl.BlockSpec(order.shape, whole),
            pl.BlockSpec(relative.shape, whole),
            pl.BlockSpec(grads.shape, whole, pipeline_mode=once),
            pl.BlockSpec((GROUP_TOK, block), column),
            pl.BlockSpec((units, slab), column),
            pl.BlockSpec((units, slab), column),
            pl.BlockSpec((units, slab), column),
        ],
        out_specs=(
            pl.BlockSpec(memory_space=pltpu.SMEM),
            pl.BlockSpec((1, units, block), lambda i: (0, 0, i)),
            pl.BlockSpec((1, units, block), lambda i: (0, 0, i)),
            pl.BlockSpec((units, slab), column),
            pl.BlockSpec((units, slab), column),
        ),
        scratch_shapes=[pltpu.VMEM((2 * units, GROUP_TOK), BF16)],
        compiler_params=pltpu.CompilerParams(dimension_semantics=("arbitrary",)),
    )(codes, order, relative, grads, x_all, average, outer_gate, moment)


def per_device(tokens, readout, resp_mask, order, w_gate, w_up, outer_gate, outer_up, moment):
    codes = jnp.asarray(position_codes())
    x_all, grads, average, relative = gather_forward(
        codes, resp_mask.reshape(1, -1), tokens, readout.T, w_gate[0], w_up[0], outer_gate, outer_up
    )
    return backward(codes, order, relative, grads, x_all, average, outer_gate, moment)


def solution(mesh):
    return jax.shard_map(
        per_device,
        mesh=mesh,
        in_specs=(
            P(("rep", "fsdp"), None),
            P("rep", "fsdp"),
            P("rep"),
            P("rep", None),
            P("rep", "fsdp", None),
            P("rep", "fsdp", None),
            P("fsdp", "rep"),
            P("fsdp", "rep"),
            P("fsdp", "rep"),
        ),
        out_specs=(
            P("rep"),
            P("rep", "fsdp", None),
            P("rep", "fsdp", None),
            P("fsdp", "rep"),
            P("fsdp", "rep"),
        ),
        check_vma=False,
    )
```

```python
import functools
import heapq

import jax
import jax.numpy as jnp
import numpy as np
from jax import lax
from jax.experimental import pallas as pl
from jax.experimental.pallas import tpu as pltpu
from jax.sharding import PartitionSpec as P

BLOCK = 128
LEN = 16
NZ, NX, NY = 8, 2, 4
SEQS = NZ * NX * NY
GROUP_TOK = SEQS * LEN
CHUNK = 256
CHUNKS = GROUP_TOK // CHUNK
PER_CHUNK = CHUNK // LEN
PIECES = 2

dpo_beta = 0.1
outer_rate = 0.7
outer_mu = 0.9
tiny_eps = 1e-06

MESH = pl.DeviceIdType.MESH
K1_LIMIT = 20 * 2**20
K2_LIMIT = 16 * 2**20
F32 = jnp.float32
BF16 = jnp.bfloat16


def gather_plan():
    arrives = {}
    flip = 0
    for dx in range(NX):
        for dz in range(NZ):
            for dy in range(NY):
                if (dx, dy, dz) == (0, 0, 0):
                    continue
                if dy == 0 and dz == 0:
                    side = "x"
                elif dz != 0 and (dy == 0 or (dx == 1 and dz != 4)):
                    side = "z+" if dz < 4 or (dz == 4 and dx == 0) else "z-"
                elif dy == 2:
                    side = "y+" if flip % 2 == 0 else "y-"
                    flip += 1
                else:
                    side = "y+" if dy == 1 else "y-"
                for p in range(PIECES):
                    arrives[(dx, dy, dz), p] = side
    for p in range(PIECES // 2):
        arrives[(1, 1, 3), p] = "y+"
        arrives[(1, 3, 5), p] = "y-"
    return arrives


ARRIVES = gather_plan()


def source(s, p):
    dx, dy, dz = s
    side = ARRIVES[s, p]
    if side == "x":
        return (dx ^ 1, dy, dz)
    if side[0] == "y":
        return (dx, (dy + (-1 if side == "y+" else 1)) % NY, dz)
    return (dx, dy, (dz + (-1 if side == "z+" else 1)) % NZ)


def gather_order(wire=2.73 / PIECES, hop=2.2, far=3.0):
    children = {}
    for s, p in ARRIVES:
        children.setdefault((source(s, p), p), []).append((s, p))

    def depth(piece):
        return 1 + max([depth(k) for k in children.get(piece, [])], default=0)

    for kids in children.values():
        kids.sort(key=lambda piece: -depth(piece))
    free = {side: 0.0 for side in ("x", "y+", "y-", "z+", "z-")}
    events = [(0.0, p, ((0, 0, 0), p)) for p in range(PIECES)]
    count = PIECES
    order = []
    while events:
        now, _, piece = heapq.heappop(events)
        order.append(piece)
        for kid in children.get(piece, []):
            side = ARRIVES[kid]
            free[side] = max(free[side], now) + wire
            heapq.heappush(events, (free[side] + (far if side == "x" else hop), count, kid))
            count += 1
    return order, children


ORDER, CHILDREN = gather_order()
RANK = {}
for _i, (_s, _) in enumerate(ORDER):
    if all(_s != later for later, _ in ORDER[_i + 1:]):
        RANK[_s] = len(RANK)


def position_codes():
    codes = np.zeros((1, GROUP_TOK), np.int32)
    for (dx, dy, dz), rank in RANK.items():
        codes[0, rank * LEN:(rank + 1) * LEN] = dz * 8 + dx * 4 + dy
    return codes


def sequence_of(codes):
    me = lax.axis_index("fsdp")
    z, x, y = me // 8, (me // 4) % 2, me % 4
    dz, dx, dy = codes >> 3, (codes >> 2) & 1, codes & 3
    return (((dz + z) & 7) << 3) + (((dx + x) & 1) << 2) + ((dy + y) & 3)


def iota(shape, axis):
    return lax.broadcasted_iota(jnp.int32, shape, axis)


def column_to_row(column, rows, lanes):
    eye = iota((rows, lanes), 0) == iota((rows, lanes), 1)
    return jnp.sum(jnp.where(eye, column, 0.0), axis=0, keepdims=True)


def row_to_column(row, rows, lanes):
    eye = iota((rows, lanes), 0) == iota((rows, lanes), 1)
    return jnp.sum(jnp.where(eye, row, 0.0), axis=1, keepdims=True)


def gather_kernel(
    codes_hbm, mask_hbm, tokens_hbm, readout_hbm, wg_hbm, wu_hbm, og_hbm, ou_hbm,
    x_all, grads, average, relative_out,
    codes_ref, mask_ref, policy, outer, own, slabs, readout, both, token_score,
    near, wide, near_own, wide_own,
    local_sem, send_sem, recv_sem, rep_send, rep_recv, sum_send, sum_recv,
):
    units, width = wg_hbm.shape
    part = own.shape[1]
    rep = lax.axis_index("rep")
    me = lax.axis_index("fsdp")
    z, x, y = me // 8, (me // 4) % 2, me % 4

    def at(dx, dy, dz):
        return ((z + dz) % 8) * 8 + ((x + dx) % 2) * 4 + (y + dy) % 4

    barrier = pltpu.get_barrier_semaphore()
    peers = [(rep, at(0, 0, d)) for d in range(1, NZ)]
    peers += [(rep, at(d // 4, d % 4, 0)) for d in range(1, NX * NY)]
    peers += [(rep ^ d, me) for d in range(1, 4)]
    for peer in peers:
        pl.semaphore_signal(barrier, inc=1, device_id=peer, device_id_type=MESH)

    def columns(r):
        return pl.ds(pl.multiple_of(r * part, part), part)

    local = [
        pltpu.make_async_copy(tokens_hbm, x_all.at[pl.ds(0, LEN), :], local_sem.at[0]),
        pltpu.make_async_copy(readout_hbm, readout, local_sem.at[1]),
        pltpu.make_async_copy(wg_hbm, policy.at[pl.ds(0, units), :], local_sem.at[2]),
        pltpu.make_async_copy(wu_hbm, policy.at[pl.ds(units, units), :], local_sem.at[3]),
        pltpu.make_async_copy(og_hbm, own, local_sem.at[4]),
        pltpu.make_async_copy(og_hbm, outer.at[pl.ds(0, units), columns(rep)], local_sem.at[5]),
        pltpu.make_async_copy(ou_hbm, outer.at[pl.ds(units, units), columns(rep)], local_sem.at[6]),
        pltpu.make_async_copy(wg_hbm.at[:, columns(rep)], slabs.at[0], local_sem.at[7]),
        pltpu.make_async_copy(codes_hbm, codes_ref, local_sem.at[8]),
        pltpu.make_async_copy(mask_hbm, mask_ref, local_sem.at[9]),
    ]
    for copy in local:
        copy.start()
    pl.semaphore_wait(barrier, len(peers))

    back = {"x": (1, 0, 0), "y+": (0, -1, 0), "y-": (0, 1, 0), "z+": (0, 0, -1), "z-": (0, 0, 1)}

    def piece_copy(s, p):
        origin = source(s, p)
        rank = RANK[s]
        lanes = pl.ds(p * (width // PIECES), width // PIECES)
        if origin == (0, 0, 0):
            src = tokens_hbm.at[:, lanes]
        else:
            src = x_all.at[pl.ds(RANK[origin] * LEN, LEN), lanes]
        return pltpu.make_async_remote_copy(
            src_ref=src,
            dst_ref=x_all.at[pl.ds(rank * LEN, LEN), lanes],
            send_sem=send_sem.at[rank * PIECES + p],
            recv_sem=recv_sem.at[rank * PIECES + p],
            device_id=(rep, at(*back[ARRIVES[s, p]])),
            device_id_type=MESH,
        )

    copies = {(s, p): piece_copy(s, p) for s, p in ARRIVES}

    def rep_copy(i, src, dst, distance):
        return pltpu.make_async_remote_copy(
            src_ref=src, dst_ref=dst, send_sem=rep_send.at[i], recv_sem=rep_recv.at[i],
            device_id=(rep ^ distance, me), device_id_type=MESH,
        )

    gate_rows, up_rows = pl.ds(0, units), pl.ds(units, units)
    mine, across = columns(rep), columns(rep ^ 2)
    gate_far = rep_copy(0, og_hbm, outer.at[gate_rows, mine], 2)
    up_far = rep_copy(1, ou_hbm, outer.at[up_rows, mine], 2)
    gate_near = rep_copy(2, og_hbm, outer.at[gate_rows, mine], 1)
    up_near = rep_copy(3, ou_hbm, outer.at[up_rows, mine], 1)
    gate_pass = rep_copy(4, outer.at[gate_rows, across], outer.at[gate_rows, across], 1)
    up_pass = rep_copy(5, outer.at[up_rows, across], outer.at[up_rows, across], 1)
    slab_copies = [
        rep_copy(5 + d, wg_hbm.at[:, columns(rep ^ d)], slabs.at[d], d) for d in (1, 2, 3)
    ]

    for p in range(PIECES):
        for piece in CHILDREN[(0, 0, 0), p]:
            copies[piece].start()
    for copy in (gate_far, gate_near, up_far, up_near, slab_copies[0], slab_copies[1], slab_copies[2]):
        copy.start()

    for i in (1, 8, 9):
        local[i].wait()
    masked = (readout[...].astype(F32) * mask_ref[...].astype(F32)).astype(BF16)
    sequence = sequence_of(codes_ref[...])
    wanted = sequence * LEN + (iota((1, GROUP_TOK), 1) & (LEN - 1))
    for c in range(CHUNKS):
        lanes = slice(c * CHUNK, (c + 1) * CHUNK)
        pick = (iota((GROUP_TOK, CHUNK), 0) == wanted[:, lanes]).astype(F32).astype(BF16)
        readout[:, lanes] = jnp.dot(masked, pick, preferred_element_type=F32).astype(BF16)
    token_score[...] = jnp.zeros_like(token_score)
    for i in (2, 3):
        local[i].wait()

    ROWS = 32
    HALF = width // 2

    def unit_project(weights, c, half):
        cols = pl.ds(half * HALF, HALF)
        product = lax.dot_general(
            weights[:, cols], x_all[pl.ds(c * CHUNK, CHUNK), cols], (((1,), (1,)), ((), ())),
            preferred_element_type=F32,
        )
        if half == 0:
            both[...] = product
        else:
            both[...] += product

    def unit_policy(c):
        lanes = pl.ds(c * CHUNK, CHUNK)

        def body(i, total):
            rows = pl.ds(pl.multiple_of(i * ROWS, ROWS), ROWS)
            upper_rows = pl.ds(pl.multiple_of(units + i * ROWS, ROWS), ROWS)
            gate, upper = both[rows, :], both[upper_rows, :]
            read = readout[rows, lanes].astype(F32)
            sigma = jax.nn.sigmoid(gate)
            silu = gate * sigma
            hidden = (silu * upper).astype(BF16).astype(F32)
            grads[rows, lanes] = read * upper * sigma * (1.0 + gate * (1.0 - sigma))
            grads[upper_rows, lanes] = read * silu
            return total + jnp.sum(hidden * read, axis=0, keepdims=True)

        total = lax.fori_loop(0, units // ROWS, body, jnp.zeros((1, CHUNK), F32))
        token_score[:, lanes] += total

    def unit_reference(c):
        lanes = pl.ds(c * CHUNK, CHUNK)

        def body(i, total):
            rows = pl.ds(pl.multiple_of(i * ROWS, ROWS), ROWS)
            upper_rows = pl.ds(pl.multiple_of(units + i * ROWS, ROWS), ROWS)
            gate, upper = both[rows, :], both[upper_rows, :]
            read = readout[rows, lanes].astype(F32)
            hidden = (gate * jax.nn.sigmoid(gate) * upper).astype(BF16).astype(F32)
            return total + jnp.sum(hidden * read, axis=0, keepdims=True)

        total = lax.fori_loop(0, units // ROWS, body, jnp.zeros((1, CHUNK), F32))
        token_score[:, lanes] -= total

    def policy_units(c):
        return [
            functools.partial(unit_project, policy, c, 0),
            functools.partial(unit_project, policy, c, 1),
            functools.partial(unit_policy, c),
        ]

    def reference_units(c):
        return [
            functools.partial(unit_project, outer, c, 0),
            functools.partial(unit_project, outer, c, 1),
            functools.partial(unit_reference, c),
        ]

    todo = []
    local[0].wait()
    left = {s: PIECES for s in RANK}
    for s, p in ORDER[PIECES:]:
        copies[s, p].wait_recv()
        for piece in CHILDREN.get((s, p), []):
            copies[piece].start()
        left[s] -= 1
        if left[s]:
            continue
        rank = RANK[s]
        if rank == 20:
            gate_far.wait_recv()
            gate_pass.start()
        if rank == 36:
            up_far.wait_recv()
            up_pass.start()
        if rank == 40:
            local[5].wait()
            local[6].wait()
            for copy in (gate_near, up_near, gate_pass, up_pass):
                copy.wait_recv()
            todo += reference_units(0) + reference_units(1)
        if rank % PER_CHUNK == PER_CHUNK - 1:
            c = rank // PER_CHUNK
            todo += policy_units(c)
            if c >= 2:
                todo += reference_units(c)
        if todo:
            todo.pop(0)()
    for unit in todo:
        unit()

    belongs = iota((SEQS, GROUP_TOK), 0) == sequence
    partial = jnp.sum(jnp.where(belongs, token_score[...], 0.0), axis=1, keepdims=True)
    partial = column_to_row(partial, SEQS, BLOCK)
    near_own[...] = partial
    near_copies = [
        pltpu.make_async_remote_copy(
            src_ref=near_own, dst_ref=near.at[z], send_sem=sum_send.at[d], recv_sem=sum_recv.at[z],
            device_id=(rep, at(0, 0, d)), device_id_type=MESH,
        )
        for d in (4, 3, 5, 2, 6, 1, 7)
    ]
    for copy in near_copies:
        copy.start()
    near[z] = partial

    for copy in slab_copies:
        copy.wait_recv()
    local[4].wait()
    local[7].wait()
    STEP = 16

    def pseudo(i, _):
        rows = pl.ds(pl.multiple_of(i * STEP, STEP), STEP)
        for b in range(part // BLOCK):
            lanes = slice(b * BLOCK, (b + 1) * BLOCK)
            own_block = own[rows, lanes].astype(F32)
            total = jnp.zeros((STEP, BLOCK), F32)
            for r in range(4):
                delta = own_block - slabs[r, rows, lanes].astype(F32)
                scale = jnp.max(jnp.abs(delta), axis=1, keepdims=True) + tiny_eps
                scale = scale.astype(BF16).astype(F32)
                total += (delta / scale).astype(BF16).astype(F32) * scale
            average[rows, lanes] = total * 0.25
        return 0

    half = units // STEP // 2
    lax.fori_loop(0, half, pseudo, 0)

    for d in range(1, NZ):
        pltpu.make_async_remote_copy(
            src_ref=near_own, dst_ref=near.at[(z + d) % 8], send_sem=sum_send.at[d],
            recv_sem=sum_recv.at[(z + d) % 8], device_id=(rep, at(0, 0, d)), device_id_type=MESH,
        ).wait_recv()
    partial = near[0]
    for i in range(1, NZ):
        partial = partial + near[i]
    plane = x * 4 + y
    wide_own[...] = partial
    wide_copies = [
        pltpu.make_async_remote_copy(
            src_ref=wide_own, dst_ref=wide.at[plane], send_sem=sum_send.at[8 + d],
            recv_sem=sum_recv.at[8 + plane], device_id=(rep, at(d // 4, d % 4, 0)), device_id_type=MESH,
        )
        for d in (6, 5, 7, 2, 4, 1, 3)
    ]
    for copy in wide_copies:
        copy.start()
    wide[plane] = partial

    lax.fori_loop(half, units // STEP, pseudo, 0)

    for d in range(1, NX * NY):
        other = ((x + d // 4) % 2) * 4 + (y + d % 4) % 4
        pltpu.make_async_remote_copy(
            src_ref=wide_own, dst_ref=wide.at[other], send_sem=sum_send.at[8 + d],
            recv_sem=sum_recv.at[8 + other], device_id=(rep, at(d // 4, d % 4, 0)), device_id_type=MESH,
        ).wait_recv()
    partial = wide[0]
    for i in range(1, NX * NY):
        partial = partial + wide[i]
    relative_out[...] = partial

    for piece in ORDER[PIECES:]:
        copies[piece].wait_send()
    for copy in (gate_far, up_far, gate_near, up_near, gate_pass, up_pass, *slab_copies):
        copy.wait_send()
    for copy in near_copies + wide_copies:
        copy.wait_send()


def gather_forward(codes, mask, tokens, readout_t, w_gate, w_up, outer_gate, outer_up):
    units, width = w_gate.shape
    part = outer_gate.shape[1]
    vmem_spec = pl.BlockSpec(memory_space=pltpu.VMEM)
    return pl.pallas_call(
        gather_kernel,
        name="gather_forward",
        out_shape=(
            jax.ShapeDtypeStruct((GROUP_TOK, width), BF16),
            jax.ShapeDtypeStruct((2 * units, GROUP_TOK), F32),
            jax.ShapeDtypeStruct((units, part), F32),
            jax.ShapeDtypeStruct((1, BLOCK), F32),
        ),
        in_specs=[pl.BlockSpec(memory_space=pltpu.HBM)] * 8,
        out_specs=(vmem_spec,) * 4,
        scratch_shapes=[
            pltpu.VMEM((1, GROUP_TOK), jnp.int32),
            pltpu.VMEM((1, GROUP_TOK), jnp.int32),
            pltpu.VMEM((2 * units, width), BF16),
            pltpu.VMEM((2 * units, width), BF16),
            pltpu.VMEM((units, part), BF16),
            pltpu.VMEM((4, units, part), BF16),
            pltpu.VMEM((units, GROUP_TOK), BF16),
            pltpu.VMEM((2 * units, CHUNK), F32),
            pltpu.VMEM((1, GROUP_TOK), F32),
            pltpu.VMEM((NZ, 1, BLOCK), F32),
            pltpu.VMEM((NX * NY, 1, BLOCK), F32),
            pltpu.VMEM((1, BLOCK), F32),
            pltpu.VMEM((1, BLOCK), F32),
            pltpu.SemaphoreType.DMA((10,)),
            pltpu.SemaphoreType.DMA((SEQS * PIECES,)),
            pltpu.SemaphoreType.DMA((SEQS * PIECES,)),
            pltpu.SemaphoreType.DMA((9,)),
            pltpu.SemaphoreType.DMA((9,)),
            pltpu.SemaphoreType.DMA((16,)),
            pltpu.SemaphoreType.DMA((16,)),
        ],
        compiler_params=pltpu.CompilerParams(
            collective_id=0, has_side_effects=True, vmem_limit_bytes=K1_LIMIT
        ),
    )(*(pltpu.with_memory_space_constraint(a, pltpu.HBM) for a in (
        codes, mask, tokens, readout_t, w_gate, w_up, outer_gate, outer_up
    )))


STEPS = 8


def backward_kernel(
    codes_ref, order_ref, relative_ref, grads, x_all, average, outer, moment,
    loss_out, gate_hbm, up_hbm, new_outer_hbm, new_moment_hbm,
    scaled, products, new_outer, new_moment, state_sem, out_sem,
):
    units = outer.shape[0]
    width = x_all.shape[1]
    block, slab = width // STEPS, outer.shape[1] // STEPS
    pairs = SEQS // 2

    relative = row_to_column(relative_ref[...], SEQS, BLOCK)
    placed = iota((SEQS, SEQS), 0) == order_ref[...]
    by_place = jnp.sum(jnp.where(placed, relative, 0.0), axis=0, keepdims=True)
    place, pair = iota((pairs, SEQS), 1), iota((pairs, SEQS), 0)
    sign = jnp.where(place == 2 * pair, 1.0, jnp.where(place == 2 * pair + 1, -1.0, 0.0))
    margin = dpo_beta * jnp.sum(sign * by_place, axis=1, keepdims=True)
    loss_out[0] = jnp.sum(jax.nn.softplus(-margin)) / pairs
    weight = dpo_beta * jax.nn.sigmoid(-margin) / pairs
    place_coef = jnp.sum(-sign * weight, axis=0, keepdims=True)
    coef = jnp.sum(jnp.where(placed, place_coef, 0.0), axis=1, keepdims=True)
    belongs = iota((SEQS, GROUP_TOK), 0) == sequence_of(codes_ref[...])
    token_grad = jnp.sum(jnp.where(belongs, coef, 0.0), axis=0, keepdims=True)
    scaled[...] = (grads[...] * token_grad).astype(BF16)

    out_copies = []
    for i in range(STEPS):
        cols = pl.ds(i * block, block)
        products[:, cols] = jnp.dot(
            scaled[...], x_all[:, cols], preferred_element_type=F32
        ).astype(BF16)
        lanes = slice(i * slab, (i + 1) * slab)
        fresh = outer_mu * moment[:, lanes] + average[:, lanes]
        new_moment[:, lanes] = fresh
        new_outer[:, lanes] = (
            outer[:, lanes].astype(F32) - outer_rate * (average[:, lanes] + outer_mu * fresh)
        ).astype(BF16)
        out_copies += [
            pltpu.make_async_copy(
                products.at[pl.ds(0, units), cols], gate_hbm.at[0, :, cols], out_sem.at[2 * i]
            ),
            pltpu.make_async_copy(
                products.at[pl.ds(units, units), cols], up_hbm.at[0, :, cols], out_sem.at[2 * i + 1]
            ),
        ]
        out_copies[-2].start()
        out_copies[-1].start()
    out_copies += [
        pltpu.make_async_copy(new_outer, new_outer_hbm, state_sem.at[0]),
        pltpu.make_async_copy(new_moment, new_moment_hbm, state_sem.at[1]),
    ]
    out_copies[-2].start()
    out_copies[-1].start()
    for copy in out_copies:
        copy.wait()


def backward(codes, order, relative, grads, x_all, average, outer_gate, moment):
    units, part = outer_gate.shape
    width = x_all.shape[1]
    any_spec = pl.BlockSpec(memory_space=pl.ANY)
    vmem_spec = pl.BlockSpec(memory_space=pltpu.VMEM)
    return pl.pallas_call(
        backward_kernel,
        name="backward",
        out_shape=(
            jax.ShapeDtypeStruct((1,), F32),
            jax.ShapeDtypeStruct((1, units, width), BF16),
            jax.ShapeDtypeStruct((1, units, width), BF16),
            jax.ShapeDtypeStruct((units, part), BF16),
            jax.ShapeDtypeStruct((units, part), F32),
        ),
        in_specs=[vmem_spec] * 8,
        out_specs=(pl.BlockSpec(memory_space=pltpu.SMEM),) + (any_spec,) * 4,
        scratch_shapes=[
            pltpu.VMEM((2 * units, GROUP_TOK), BF16),
            pltpu.VMEM((2 * units, width), BF16),
            pltpu.VMEM((units, part), BF16),
            pltpu.VMEM((units, part), F32),
            pltpu.SemaphoreType.DMA((2,)),
            pltpu.SemaphoreType.DMA((2 * STEPS,)),
        ],
        compiler_params=pltpu.CompilerParams(vmem_limit_bytes=K2_LIMIT),
    )(codes, order, relative, grads, x_all, average, outer_gate, moment)


def per_device(tokens, readout, resp_mask, order, w_gate, w_up, outer_gate, outer_up, moment):
    codes = jnp.asarray(position_codes())
    x_all, grads, average, relative = gather_forward(
        codes, resp_mask.reshape(1, -1), tokens, readout.T, w_gate[0], w_up[0], outer_gate, outer_up
    )
    return backward(codes, order, relative, grads, x_all, average, outer_gate, moment)


def solution(mesh):
    return jax.shard_map(
        per_device,
        mesh=mesh,
        in_specs=(
            P(("rep", "fsdp"), None),
            P("rep", "fsdp"),
            P("rep"),
            P("rep", None),
            P("rep", "fsdp", None),
            P("rep", "fsdp", None),
            P("fsdp", "rep"),
            P("fsdp", "rep"),
            P("fsdp", "rep"),
        ),
        out_specs=(
            P("rep"),
            P("rep", "fsdp", None),
            P("rep", "fsdp", None),
            P("fsdp", "rep"),
            P("fsdp", "rep"),
        ),
        check_vma=False,
    )
```

```python
import functools
import heapq

import jax
import jax.numpy as jnp
import numpy as np
from jax import lax
from jax.experimental import pallas as pl
from jax.experimental.pallas import tpu as pltpu
from jax.sharding import PartitionSpec as P

BLOCK = 128
LEN = 16
NZ, NX, NY = 8, 2, 4
SEQS = NZ * NX * NY
GROUP_TOK = SEQS * LEN
CHUNKS = ((0, 256), (256, 256), (512, 256), (768, 128), (896, 128))
PIECES = 2

dpo_beta = 0.1
outer_rate = 0.7
outer_mu = 0.9
tiny_eps = 1e-06

MESH = pl.DeviceIdType.MESH
K1_LIMIT = 20 * 2**20
K2_LIMIT = 16 * 2**20
F32 = jnp.float32
BF16 = jnp.bfloat16


def gather_plan():
    arrives = {}
    flip = 0
    for dx in range(NX):
        for dz in range(NZ):
            for dy in range(NY):
                if (dx, dy, dz) == (0, 0, 0):
                    continue
                if dy == 0 and dz == 0:
                    side = "x"
                elif dz != 0 and (dy == 0 or (dx == 1 and dz != 4)):
                    side = "z+" if dz < 4 or (dz == 4 and dx == 0) else "z-"
                elif dy == 2:
                    side = "y+" if flip % 2 == 0 else "y-"
                    flip += 1
                else:
                    side = "y+" if dy == 1 else "y-"
                for p in range(PIECES):
                    arrives[(dx, dy, dz), p] = side
    for p in range(PIECES // 2):
        arrives[(1, 1, 3), p] = "y+"
        arrives[(1, 3, 5), p] = "y-"
    return arrives


ARRIVES = gather_plan()


def source(s, p):
    dx, dy, dz = s
    side = ARRIVES[s, p]
    if side == "x":
        return (dx ^ 1, dy, dz)
    if side[0] == "y":
        return (dx, (dy + (-1 if side == "y+" else 1)) % NY, dz)
    return (dx, dy, (dz + (-1 if side == "z+" else 1)) % NZ)


def gather_order(wire=2.73 / PIECES, hop=2.2, far=3.0):
    children = {}
    for s, p in ARRIVES:
        children.setdefault((source(s, p), p), []).append((s, p))

    def depth(piece):
        return 1 + max([depth(k) for k in children.get(piece, [])], default=0)

    for kids in children.values():
        kids.sort(key=lambda piece: -depth(piece))
    free = {side: 0.0 for side in ("x", "y+", "y-", "z+", "z-")}
    events = [(0.0, p, ((0, 0, 0), p)) for p in range(PIECES)]
    count = PIECES
    order = []
    while events:
        now, _, piece = heapq.heappop(events)
        order.append(piece)
        for kid in children.get(piece, []):
            side = ARRIVES[kid]
            free[side] = max(free[side], now) + wire
            heapq.heappush(events, (free[side] + (far if side == "x" else hop), count, kid))
            count += 1
    return order, children


ORDER, CHILDREN = gather_order()
RANK = {}
for _i, (_s, _) in enumerate(ORDER):
    if all(_s != later for later, _ in ORDER[_i + 1:]):
        RANK[_s] = len(RANK)


def position_codes():
    codes = np.zeros((1, GROUP_TOK), np.int32)
    for (dx, dy, dz), rank in RANK.items():
        codes[0, rank * LEN:(rank + 1) * LEN] = dz * 8 + dx * 4 + dy
    return codes


def sequence_of(codes):
    me = lax.axis_index("fsdp")
    z, x, y = me // 8, (me // 4) % 2, me % 4
    dz, dx, dy = codes >> 3, (codes >> 2) & 1, codes & 3
    return (((dz + z) & 7) << 3) + (((dx + x) & 1) << 2) + ((dy + y) & 3)


def iota(shape, axis):
    return lax.broadcasted_iota(jnp.int32, shape, axis)


def column_to_row(column, rows, lanes):
    eye = iota((rows, lanes), 0) == iota((rows, lanes), 1)
    return jnp.sum(jnp.where(eye, column, 0.0), axis=0, keepdims=True)


def row_to_column(row, rows, lanes):
    eye = iota((rows, lanes), 0) == iota((rows, lanes), 1)
    return jnp.sum(jnp.where(eye, row, 0.0), axis=1, keepdims=True)


def gather_kernel(
    codes_hbm, mask_hbm, tokens_hbm, readout_hbm, wg_hbm, wu_hbm, og_hbm, ou_hbm,
    x_all, grads, average, relative_out,
    codes_ref, mask_ref, policy, outer, own, slabs, readout, both, token_score,
    near, wide, near_own, wide_own,
    local_sem, send_sem, recv_sem, rep_send, rep_recv, sum_send, sum_recv,
):
    units, width = wg_hbm.shape
    part = own.shape[1]
    rep = lax.axis_index("rep")
    me = lax.axis_index("fsdp")
    z, x, y = me // 8, (me // 4) % 2, me % 4

    def at(dx, dy, dz):
        return ((z + dz) % 8) * 8 + ((x + dx) % 2) * 4 + (y + dy) % 4

    barrier = pltpu.get_barrier_semaphore()
    peers = [(rep, at(*side)) for side in ((0, 0, 1), (0, 0, -1), (0, 1, 0), (0, -1, 0), (1, 0, 0))]
    peers += [(rep ^ d, me) for d in range(1, 4)]
    for peer in peers:
        pl.semaphore_signal(barrier, inc=1, device_id=peer, device_id_type=MESH)

    def columns(r):
        return pl.ds(pl.multiple_of(r * part, part), part)

    local = [
        pltpu.make_async_copy(tokens_hbm, x_all.at[pl.ds(0, LEN), :], local_sem.at[0]),
        pltpu.make_async_copy(readout_hbm, readout, local_sem.at[1]),
        pltpu.make_async_copy(wg_hbm, policy.at[pl.ds(0, units), :], local_sem.at[2]),
        pltpu.make_async_copy(wu_hbm, policy.at[pl.ds(units, units), :], local_sem.at[3]),
        pltpu.make_async_copy(og_hbm, own, local_sem.at[4]),
        pltpu.make_async_copy(og_hbm, outer.at[pl.ds(0, units), columns(rep)], local_sem.at[5]),
        pltpu.make_async_copy(ou_hbm, outer.at[pl.ds(units, units), columns(rep)], local_sem.at[6]),
        pltpu.make_async_copy(wg_hbm.at[:, columns(rep)], slabs.at[0], local_sem.at[7]),
        pltpu.make_async_copy(codes_hbm, codes_ref, local_sem.at[8]),
        pltpu.make_async_copy(mask_hbm, mask_ref, local_sem.at[9]),
    ]
    for copy in local:
        copy.start()
    pl.semaphore_wait(barrier, len(peers))

    back = {"x": (1, 0, 0), "y+": (0, -1, 0), "y-": (0, 1, 0), "z+": (0, 0, -1), "z-": (0, 0, 1)}

    def piece_copy(s, p):
        origin = source(s, p)
        rank = RANK[s]
        lanes = pl.ds(p * (width // PIECES), width // PIECES)
        if origin == (0, 0, 0):
            src = tokens_hbm.at[:, lanes]
        else:
            src = x_all.at[pl.ds(RANK[origin] * LEN, LEN), lanes]
        return pltpu.make_async_remote_copy(
            src_ref=src,
            dst_ref=x_all.at[pl.ds(rank * LEN, LEN), lanes],
            send_sem=send_sem.at[rank * PIECES + p],
            recv_sem=recv_sem.at[rank * PIECES + p],
            device_id=(rep, at(*back[ARRIVES[s, p]])),
            device_id_type=MESH,
        )

    copies = {(s, p): piece_copy(s, p) for s, p in ARRIVES}

    def rep_copy(i, src, dst, distance):
        return pltpu.make_async_remote_copy(
            src_ref=src, dst_ref=dst, send_sem=rep_send.at[i], recv_sem=rep_recv.at[i],
            device_id=(rep ^ distance, me), device_id_type=MESH,
        )

    gate_rows, up_rows = pl.ds(0, units), pl.ds(units, units)
    mine, across = columns(rep), columns(rep ^ 2)
    gate_far = rep_copy(0, og_hbm, outer.at[gate_rows, mine], 2)
    up_far = rep_copy(1, ou_hbm, outer.at[up_rows, mine], 2)
    gate_near = rep_copy(2, og_hbm, outer.at[gate_rows, mine], 1)
    up_near = rep_copy(3, ou_hbm, outer.at[up_rows, mine], 1)
    gate_pass = rep_copy(4, outer.at[gate_rows, across], outer.at[gate_rows, across], 1)
    up_pass = rep_copy(5, outer.at[up_rows, across], outer.at[up_rows, across], 1)
    slab_copies = [
        rep_copy(5 + d, wg_hbm.at[:, columns(rep ^ d)], slabs.at[d], d) for d in (1, 2, 3)
    ]

    for p in range(PIECES):
        for piece in CHILDREN[(0, 0, 0), p]:
            copies[piece].start()
    for copy in (gate_far, gate_near, up_far, up_near, slab_copies[0], slab_copies[1], slab_copies[2]):
        copy.start()

    for i in (1, 8, 9):
        local[i].wait()
    masked = (readout[...].astype(F32) * mask_ref[...].astype(F32)).astype(BF16)
    sequence = sequence_of(codes_ref[...])
    wanted = sequence * LEN + (iota((1, GROUP_TOK), 1) & (LEN - 1))
    for start in range(0, GROUP_TOK, 256):
        lanes = slice(start, start + 256)
        pick = (iota((GROUP_TOK, 256), 0) == wanted[:, lanes]).astype(F32).astype(BF16)
        readout[:, lanes] = jnp.dot(masked, pick, preferred_element_type=F32).astype(BF16)
    token_score[...] = jnp.zeros_like(token_score)
    for i in (2, 3):
        local[i].wait()

    ROWS = 32

    def unit_project(weights, rows, c):
        start, size = CHUNKS[c]
        both[rows, pl.ds(0, size)] = lax.dot_general(
            weights[rows, :], x_all[pl.ds(start, size), :], (((1,), (1,)), ((), ())),
            preferred_element_type=F32,
        )

    def unit_policy(c):
        start, size = CHUNKS[c]
        lanes, used = pl.ds(start, size), pl.ds(0, size)

        def body(i, total):
            rows = pl.ds(pl.multiple_of(i * ROWS, ROWS), ROWS)
            upper_rows = pl.ds(pl.multiple_of(units + i * ROWS, ROWS), ROWS)
            gate, upper = both[rows, used], both[upper_rows, used]
            read = readout[rows, lanes].astype(F32)
            sigma = jax.nn.sigmoid(gate)
            silu = gate * sigma
            hidden = (silu * upper).astype(BF16).astype(F32)
            grads[rows, lanes] = read * upper * sigma * (1.0 + gate * (1.0 - sigma))
            grads[upper_rows, lanes] = read * silu
            return total + jnp.sum(hidden * read, axis=0, keepdims=True)

        total = lax.fori_loop(0, units // ROWS, body, jnp.zeros((1, size), F32))
        token_score[:, lanes] += total

    def unit_reference(c):
        start, size = CHUNKS[c]
        lanes, used = pl.ds(start, size), pl.ds(0, size)

        def body(i, total):
            rows = pl.ds(pl.multiple_of(i * ROWS, ROWS), ROWS)
            upper_rows = pl.ds(pl.multiple_of(units + i * ROWS, ROWS), ROWS)
            gate, upper = both[rows, used], both[upper_rows, used]
            read = readout[rows, lanes].astype(F32)
            hidden = (gate * jax.nn.sigmoid(gate) * upper).astype(BF16).astype(F32)
            return total + jnp.sum(hidden * read, axis=0, keepdims=True)

        total = lax.fori_loop(0, units // ROWS, body, jnp.zeros((1, size), F32))
        token_score[:, lanes] -= total

    def policy_units(c):
        return [
            functools.partial(unit_project, policy, gate_rows, c),
            functools.partial(unit_project, policy, up_rows, c),
            functools.partial(unit_policy, c),
        ]

    def reference_units(c):
        return [
            functools.partial(unit_project, outer, gate_rows, c),
            functools.partial(unit_project, outer, up_rows, c),
            functools.partial(unit_reference, c),
        ]

    todo = []
    local[0].wait()
    left = {s: PIECES for s in RANK}
    for s, p in ORDER[PIECES:]:
        copies[s, p].wait_recv()
        for piece in CHILDREN.get((s, p), []):
            copies[piece].start()
        left[s] -= 1
        if left[s]:
            continue
        rank = RANK[s]
        if rank == 19:
            gate_far.wait_recv()
            gate_pass.start()
        if rank == 33:
            up_far.wait_recv()
            up_pass.start()
        if rank == 37:
            local[5].wait()
            local[6].wait()
            for copy in (gate_near, up_near, gate_pass, up_pass):
                copy.wait_recv()
            todo += reference_units(0) + reference_units(1)
        for c, (start, size) in enumerate(CHUNKS):
            if (rank + 1) * LEN != start + size:
                continue
            todo += policy_units(c)
            if c >= 2:
                todo += reference_units(c)
        if todo:
            todo.pop(0)()
    for unit in todo:
        unit()

    belongs = iota((SEQS, GROUP_TOK), 0) == sequence
    partial = jnp.sum(jnp.where(belongs, token_score[...], 0.0), axis=1, keepdims=True)
    partial = column_to_row(partial, SEQS, BLOCK)
    near_own[...] = partial
    near_copies = [
        pltpu.make_async_remote_copy(
            src_ref=near_own, dst_ref=near.at[z], send_sem=sum_send.at[d], recv_sem=sum_recv.at[z],
            device_id=(rep, at(0, 0, d)), device_id_type=MESH,
        )
        for d in (4, 3, 5, 2, 6, 1, 7)
    ]
    for copy in near_copies:
        copy.start()
    near[z] = partial

    for copy in slab_copies:
        copy.wait_recv()
    local[4].wait()
    local[7].wait()
    STEP = 16

    def pseudo(i, _):
        rows = pl.ds(pl.multiple_of(i * STEP, STEP), STEP)
        for b in range(part // BLOCK):
            lanes = slice(b * BLOCK, (b + 1) * BLOCK)
            own_block = own[rows, lanes].astype(F32)
            total = jnp.zeros((STEP, BLOCK), F32)
            for r in range(4):
                delta = own_block - slabs[r, rows, lanes].astype(F32)
                scale = jnp.max(jnp.abs(delta), axis=1, keepdims=True) + tiny_eps
                scale = scale.astype(BF16).astype(F32)
                total += (delta / scale).astype(BF16).astype(F32) * scale
            average[rows, lanes] = total * 0.25
        return 0

    half = units // STEP // 2
    lax.fori_loop(0, half, pseudo, 0)

    for d in range(1, NZ):
        pltpu.make_async_remote_copy(
            src_ref=near_own, dst_ref=near.at[(z + d) % 8], send_sem=sum_send.at[d],
            recv_sem=sum_recv.at[(z + d) % 8], device_id=(rep, at(0, 0, d)), device_id_type=MESH,
        ).wait_recv()
    partial = near[0]
    for i in range(1, NZ):
        partial = partial + near[i]
    plane = x * 4 + y
    wide_own[...] = partial
    wide_copies = [
        pltpu.make_async_remote_copy(
            src_ref=wide_own, dst_ref=wide.at[plane], send_sem=sum_send.at[8 + d],
            recv_sem=sum_recv.at[8 + plane], device_id=(rep, at(d // 4, d % 4, 0)), device_id_type=MESH,
        )
        for d in (6, 5, 7, 2, 4, 1, 3)
    ]
    for copy in wide_copies:
        copy.start()
    wide[plane] = partial

    lax.fori_loop(half, units // STEP, pseudo, 0)

    for d in range(1, NX * NY):
        other = ((x + d // 4) % 2) * 4 + (y + d % 4) % 4
        pltpu.make_async_remote_copy(
            src_ref=wide_own, dst_ref=wide.at[other], send_sem=sum_send.at[8 + d],
            recv_sem=sum_recv.at[8 + other], device_id=(rep, at(d // 4, d % 4, 0)), device_id_type=MESH,
        ).wait_recv()
    partial = wide[0]
    for i in range(1, NX * NY):
        partial = partial + wide[i]
    relative_out[...] = partial

    for piece in ORDER[PIECES:]:
        copies[piece].wait_send()
    for copy in (gate_far, up_far, gate_near, up_near, gate_pass, up_pass, *slab_copies):
        copy.wait_send()
    for copy in near_copies + wide_copies:
        copy.wait_send()


def gather_forward(codes, mask, tokens, readout_t, w_gate, w_up, outer_gate, outer_up):
    units, width = w_gate.shape
    part = outer_gate.shape[1]
    vmem_spec = pl.BlockSpec(memory_space=pltpu.VMEM)
    return pl.pallas_call(
        gather_kernel,
        name="gather_forward",
        out_shape=(
            jax.ShapeDtypeStruct((GROUP_TOK, width), BF16),
            jax.ShapeDtypeStruct((2 * units, GROUP_TOK), F32),
            jax.ShapeDtypeStruct((units, part), F32),
            jax.ShapeDtypeStruct((1, BLOCK), F32),
        ),
        in_specs=[pl.BlockSpec(memory_space=pltpu.HBM)] * 8,
        out_specs=(vmem_spec,) * 4,
        scratch_shapes=[
            pltpu.VMEM((1, GROUP_TOK), jnp.int32),
            pltpu.VMEM((1, GROUP_TOK), jnp.int32),
            pltpu.VMEM((2 * units, width), BF16),
            pltpu.VMEM((2 * units, width), BF16),
            pltpu.VMEM((units, part), BF16),
            pltpu.VMEM((4, units, part), BF16),
            pltpu.VMEM((units, GROUP_TOK), BF16),
            pltpu.VMEM((2 * units, 256), F32),
            pltpu.VMEM((1, GROUP_TOK), F32),
            pltpu.VMEM((NZ, 1, BLOCK), F32),
            pltpu.VMEM((NX * NY, 1, BLOCK), F32),
            pltpu.VMEM((1, BLOCK), F32),
            pltpu.VMEM((1, BLOCK), F32),
            pltpu.SemaphoreType.DMA((10,)),
            pltpu.SemaphoreType.DMA((SEQS * PIECES,)),
            pltpu.SemaphoreType.DMA((SEQS * PIECES,)),
            pltpu.SemaphoreType.DMA((9,)),
            pltpu.SemaphoreType.DMA((9,)),
            pltpu.SemaphoreType.DMA((16,)),
            pltpu.SemaphoreType.DMA((16,)),
        ],
        compiler_params=pltpu.CompilerParams(
            collective_id=0, has_side_effects=True, vmem_limit_bytes=K1_LIMIT
        ),
    )(*(pltpu.with_memory_space_constraint(a, pltpu.HBM) for a in (
        codes, mask, tokens, readout_t, w_gate, w_up, outer_gate, outer_up
    )))


STEPS = 8


def backward_kernel(
    codes_ref, order_ref, relative_ref, grads, x_all, average, outer, moment,
    loss_out, gate_hbm, up_hbm, new_outer_hbm, new_moment_hbm,
    scaled, products, new_outer, new_moment, state_sem, out_sem,
):
    units = outer.shape[0]
    width = x_all.shape[1]
    block, slab = width // STEPS, outer.shape[1] // STEPS
    pairs = SEQS // 2

    relative = row_to_column(relative_ref[...], SEQS, BLOCK)
    placed = iota((SEQS, SEQS), 0) == order_ref[...]
    by_place = jnp.sum(jnp.where(placed, relative, 0.0), axis=0, keepdims=True)
    place, pair = iota((pairs, SEQS), 1), iota((pairs, SEQS), 0)
    sign = jnp.where(place == 2 * pair, 1.0, jnp.where(place == 2 * pair + 1, -1.0, 0.0))
    margin = dpo_beta * jnp.sum(sign * by_place, axis=1, keepdims=True)
    loss_out[0] = jnp.sum(jax.nn.softplus(-margin)) / pairs
    weight = dpo_beta * jax.nn.sigmoid(-margin) / pairs
    place_coef = jnp.sum(-sign * weight, axis=0, keepdims=True)
    coef = jnp.sum(jnp.where(placed, place_coef, 0.0), axis=1, keepdims=True)
    belongs = iota((SEQS, GROUP_TOK), 0) == sequence_of(codes_ref[...])
    token_grad = jnp.sum(jnp.where(belongs, coef, 0.0), axis=0, keepdims=True)
    scaled[...] = (grads[...] * token_grad).astype(BF16)

    out_copies = []
    for i in range(STEPS):
        cols = pl.ds(i * block, block)
        products[:, cols] = jnp.dot(
            scaled[...], x_all[:, cols], preferred_element_type=F32
        ).astype(BF16)
        lanes = slice(i * slab, (i + 1) * slab)
        fresh = outer_mu * moment[:, lanes] + average[:, lanes]
        new_moment[:, lanes] = fresh
        new_outer[:, lanes] = (
            outer[:, lanes].astype(F32) - outer_rate * (average[:, lanes] + outer_mu * fresh)
        ).astype(BF16)
        out_copies += [
            pltpu.make_async_copy(
                products.at[pl.ds(0, units), cols], gate_hbm.at[0, :, cols], out_sem.at[2 * i]
            ),
            pltpu.make_async_copy(
                products.at[pl.ds(units, units), cols], up_hbm.at[0, :, cols], out_sem.at[2 * i + 1]
            ),
        ]
        out_copies[-2].start()
        out_copies[-1].start()
    out_copies += [
        pltpu.make_async_copy(new_outer, new_outer_hbm, state_sem.at[0]),
        pltpu.make_async_copy(new_moment, new_moment_hbm, state_sem.at[1]),
    ]
    out_copies[-2].start()
    out_copies[-1].start()
    for copy in out_copies:
        copy.wait()


def backward(codes, order, relative, grads, x_all, average, outer_gate, moment):
    units, part = outer_gate.shape
    width = x_all.shape[1]
    any_spec = pl.BlockSpec(memory_space=pl.ANY)
    vmem_spec = pl.BlockSpec(memory_space=pltpu.VMEM)
    return pl.pallas_call(
        backward_kernel,
        name="backward",
        out_shape=(
            jax.ShapeDtypeStruct((1,), F32),
            jax.ShapeDtypeStruct((1, units, width), BF16),
            jax.ShapeDtypeStruct((1, units, width), BF16),
            jax.ShapeDtypeStruct((units, part), BF16),
            jax.ShapeDtypeStruct((units, part), F32),
        ),
        in_specs=[vmem_spec] * 8,
        out_specs=(pl.BlockSpec(memory_space=pltpu.SMEM),) + (any_spec,) * 4,
        scratch_shapes=[
            pltpu.VMEM((2 * units, GROUP_TOK), BF16),
            pltpu.VMEM((2 * units, width), BF16),
            pltpu.VMEM((units, part), BF16),
            pltpu.VMEM((units, part), F32),
            pltpu.SemaphoreType.DMA((2,)),
            pltpu.SemaphoreType.DMA((2 * STEPS,)),
        ],
        compiler_params=pltpu.CompilerParams(vmem_limit_bytes=K2_LIMIT),
    )(codes, order, relative, grads, x_all, average, outer_gate, moment)


def per_device(tokens, readout, resp_mask, order, w_gate, w_up, outer_gate, outer_up, moment):
    codes = jnp.asarray(position_codes())
    x_all, grads, average, relative = gather_forward(
        codes, resp_mask.reshape(1, -1), tokens, readout.T, w_gate[0], w_up[0], outer_gate, outer_up
    )
    return backward(codes, order, relative, grads, x_all, average, outer_gate, moment)


def solution(mesh):
    return jax.shard_map(
        per_device,
        mesh=mesh,
        in_specs=(
            P(("rep", "fsdp"), None),
            P("rep", "fsdp"),
            P("rep"),
            P("rep", None),
            P("rep", "fsdp", None),
            P("rep", "fsdp", None),
            P("fsdp", "rep"),
            P("fsdp", "rep"),
            P("fsdp", "rep"),
        ),
        out_specs=(
            P("rep"),
            P("rep", "fsdp", None),
            P("rep", "fsdp", None),
            P("fsdp", "rep"),
            P("fsdp", "rep"),
        ),
        check_vma=False,
    )
```

```python
import functools
import heapq

import jax
import jax.numpy as jnp
import numpy as np
from jax import lax
from jax.experimental import pallas as pl
from jax.experimental.pallas import tpu as pltpu
from jax.sharding import PartitionSpec as P

BLOCK = 128
LEN = 16
NZ, NX, NY = 8, 2, 4
SEQS = NZ * NX * NY
GROUP_TOK = SEQS * LEN
CHUNKS = ((0, 256), (256, 256), (512, 256), (768, 128), (896, 128))
PIECES = 2

dpo_beta = 0.1
outer_rate = 0.7
outer_mu = 0.9
tiny_eps = 1e-06

MESH = pl.DeviceIdType.MESH
K1_LIMIT = 20 * 2**20
K2_LIMIT = 16 * 2**20
F32 = jnp.float32
BF16 = jnp.bfloat16


def gather_plan():
    arrives = {}
    flip = 0
    for dx in range(NX):
        for dz in range(NZ):
            for dy in range(NY):
                if (dx, dy, dz) == (0, 0, 0):
                    continue
                if dy == 0 and dz == 0:
                    side = "x"
                elif dz != 0 and (dy == 0 or (dx == 1 and dz != 4)):
                    side = "z+" if dz < 4 or (dz == 4 and dx == 0) else "z-"
                elif dy == 2:
                    side = "y+" if flip % 2 == 0 else "y-"
                    flip += 1
                else:
                    side = "y+" if dy == 1 else "y-"
                for p in range(PIECES):
                    arrives[(dx, dy, dz), p] = side
    for p in range(PIECES // 2):
        arrives[(1, 1, 3), p] = "y+"
        arrives[(1, 3, 5), p] = "y-"
    return arrives


ARRIVES = gather_plan()


def source(s, p):
    dx, dy, dz = s
    side = ARRIVES[s, p]
    if side == "x":
        return (dx ^ 1, dy, dz)
    if side[0] == "y":
        return (dx, (dy + (-1 if side == "y+" else 1)) % NY, dz)
    return (dx, dy, (dz + (-1 if side == "z+" else 1)) % NZ)


def gather_order(wire=2.73 / PIECES, hop=2.2, far=3.0):
    children = {}
    for s, p in ARRIVES:
        children.setdefault((source(s, p), p), []).append((s, p))

    def depth(piece):
        return 1 + max([depth(k) for k in children.get(piece, [])], default=0)

    for kids in children.values():
        kids.sort(key=lambda piece: -depth(piece))
    free = {side: 0.0 for side in ("x", "y+", "y-", "z+", "z-")}
    events = [(0.0, p, ((0, 0, 0), p)) for p in range(PIECES)]
    count = PIECES
    order = []
    while events:
        now, _, piece = heapq.heappop(events)
        order.append(piece)
        for kid in children.get(piece, []):
            side = ARRIVES[kid]
            free[side] = max(free[side], now) + wire
            heapq.heappush(events, (free[side] + (far if side == "x" else hop), count, kid))
            count += 1
    return order, children


ORDER, CHILDREN = gather_order()
RANK = {}
for _i, (_s, _) in enumerate(ORDER):
    if all(_s != later for later, _ in ORDER[_i + 1:]):
        RANK[_s] = len(RANK)


def position_codes():
    codes = np.zeros((1, GROUP_TOK), np.int32)
    for (dx, dy, dz), rank in RANK.items():
        codes[0, rank * LEN:(rank + 1) * LEN] = dz * 8 + dx * 4 + dy
    return codes


def sequence_of(codes):
    me = lax.axis_index("fsdp")
    z, x, y = me // 8, (me // 4) % 2, me % 4
    dz, dx, dy = codes >> 3, (codes >> 2) & 1, codes & 3
    return (((dz + z) & 7) << 3) + (((dx + x) & 1) << 2) + ((dy + y) & 3)


def iota(shape, axis):
    return lax.broadcasted_iota(jnp.int32, shape, axis)


def column_to_row(column, rows, lanes):
    eye = iota((rows, lanes), 0) == iota((rows, lanes), 1)
    return jnp.sum(jnp.where(eye, column, 0.0), axis=0, keepdims=True)


def row_to_column(row, rows, lanes):
    eye = iota((rows, lanes), 0) == iota((rows, lanes), 1)
    return jnp.sum(jnp.where(eye, row, 0.0), axis=1, keepdims=True)


def gather_kernel(
    codes_hbm, mask_hbm, tokens_hbm, readout_hbm, wg_hbm, wu_hbm, og_hbm, ou_hbm,
    x_all, grads, average, relative_out,
    codes_ref, mask_ref, policy, outer, own, slabs, readout, masked, both, token_score,
    scores, own_score,
    local_sem, send_sem, recv_sem, rep_send, rep_recv, sum_send, sum_recv,
):
    units, width = wg_hbm.shape
    part = own.shape[1]
    rep = lax.axis_index("rep")
    me = lax.axis_index("fsdp")
    z, x, y = me // 8, (me // 4) % 2, me % 4

    def at(dx, dy, dz):
        return ((z + dz) % 8) * 8 + ((x + dx) % 2) * 4 + (y + dy) % 4

    barrier = pltpu.get_barrier_semaphore()
    peers = [(rep, at(*side)) for side in ((0, 0, 1), (0, 0, -1), (0, 1, 0), (0, -1, 0), (1, 0, 0))]
    peers += [(rep ^ d, me) for d in range(1, 4)]
    for peer in peers:
        pl.semaphore_signal(barrier, inc=1, device_id=peer, device_id_type=MESH)

    def columns(r):
        return pl.ds(pl.multiple_of(r * part, part), part)

    local = [
        pltpu.make_async_copy(tokens_hbm, x_all.at[pl.ds(0, LEN), :], local_sem.at[0]),
        pltpu.make_async_copy(readout_hbm, readout, local_sem.at[1]),
        pltpu.make_async_copy(wg_hbm, policy.at[pl.ds(0, units), :], local_sem.at[2]),
        pltpu.make_async_copy(wu_hbm, policy.at[pl.ds(units, units), :], local_sem.at[3]),
        pltpu.make_async_copy(og_hbm, own, local_sem.at[4]),
        pltpu.make_async_copy(og_hbm, outer.at[pl.ds(0, units), columns(rep)], local_sem.at[5]),
        pltpu.make_async_copy(ou_hbm, outer.at[pl.ds(units, units), columns(rep)], local_sem.at[6]),
        pltpu.make_async_copy(wg_hbm.at[:, columns(rep)], slabs.at[0], local_sem.at[7]),
        pltpu.make_async_copy(codes_hbm, codes_ref, local_sem.at[8]),
        pltpu.make_async_copy(mask_hbm, mask_ref, local_sem.at[9]),
    ]
    for copy in local:
        copy.start()
    pl.semaphore_wait(barrier, len(peers))

    back = {"x": (1, 0, 0), "y+": (0, -1, 0), "y-": (0, 1, 0), "z+": (0, 0, -1), "z-": (0, 0, 1)}

    def piece_copy(s, p):
        origin = source(s, p)
        rank = RANK[s]
        lanes = pl.ds(p * (width // PIECES), width // PIECES)
        if origin == (0, 0, 0):
            src = tokens_hbm.at[:, lanes]
        else:
            src = x_all.at[pl.ds(RANK[origin] * LEN, LEN), lanes]
        return pltpu.make_async_remote_copy(
            src_ref=src,
            dst_ref=x_all.at[pl.ds(rank * LEN, LEN), lanes],
            send_sem=send_sem.at[rank * PIECES + p],
            recv_sem=recv_sem.at[rank * PIECES + p],
            device_id=(rep, at(*back[ARRIVES[s, p]])),
            device_id_type=MESH,
        )

    copies = {(s, p): piece_copy(s, p) for s, p in ARRIVES}

    def rep_copy(i, src, dst, distance):
        return pltpu.make_async_remote_copy(
            src_ref=src, dst_ref=dst, send_sem=rep_send.at[i], recv_sem=rep_recv.at[i],
            device_id=(rep ^ distance, me), device_id_type=MESH,
        )

    gate_rows, up_rows = pl.ds(0, units), pl.ds(units, units)
    mine, across = columns(rep), columns(rep ^ 2)
    gate_far = rep_copy(0, og_hbm, outer.at[gate_rows, mine], 2)
    up_far = rep_copy(1, ou_hbm, outer.at[up_rows, mine], 2)
    gate_near = rep_copy(2, og_hbm, outer.at[gate_rows, mine], 1)
    up_near = rep_copy(3, ou_hbm, outer.at[up_rows, mine], 1)
    gate_pass = rep_copy(4, outer.at[gate_rows, across], outer.at[gate_rows, across], 1)
    up_pass = rep_copy(5, outer.at[up_rows, across], outer.at[up_rows, across], 1)
    slab_copies = [
        rep_copy(5 + d, wg_hbm.at[:, columns(rep ^ d)], slabs.at[d], d) for d in (1, 2, 3)
    ]

    for p in range(PIECES):
        for piece in CHILDREN[(0, 0, 0), p]:
            copies[piece].start()
    for copy in (gate_far, gate_near, up_far, up_near, slab_copies[0], slab_copies[1], slab_copies[2]):
        copy.start()

    for i in (1, 8, 9):
        local[i].wait()
    sequence = sequence_of(codes_ref[...])
    wanted = sequence * LEN + (iota((1, GROUP_TOK), 1) & (LEN - 1))

    def unit_mask():
        masked[...] = (readout[...].astype(F32) * mask_ref[...].astype(F32)).astype(BF16)

    def unit_order(start):
        lanes = slice(start, start + 256)
        pick = (iota((GROUP_TOK, 256), 0) == wanted[:, lanes]).astype(F32).astype(BF16)
        readout[:, lanes] = jnp.dot(masked[...], pick, preferred_element_type=F32).astype(BF16)

    token_score[...] = jnp.zeros_like(token_score)
    for i in (2, 3):
        local[i].wait()

    ROWS = 32

    def unit_project(weights, rows, c):
        start, size = CHUNKS[c]
        both[rows, pl.ds(0, size)] = lax.dot_general(
            weights[rows, :], x_all[pl.ds(start, size), :], (((1,), (1,)), ((), ())),
            preferred_element_type=F32,
        )

    LAST = len(CHUNKS) - 1
    HALF = width // 2

    def unit_half(weights, rows, lanes, half):
        start, size = CHUNKS[LAST]
        cols = pl.ds(half * HALF, HALF)
        product = lax.dot_general(
            weights[rows, cols], x_all[pl.ds(start, size), cols], (((1,), (1,)), ((), ())),
            preferred_element_type=F32,
        )
        if half == 0:
            both[rows, lanes] = product
        else:
            both[rows, lanes] += product

    def last_halves(half):
        return [
            functools.partial(unit_half, weights, rows, pl.ds(first, CHUNKS[LAST][1]), half)
            for weights, first in ((policy, 0), (outer, 128))
            for rows in (gate_rows, up_rows)
        ]

    def unit_policy(c):
        start, size = CHUNKS[c]
        lanes, used = pl.ds(start, size), pl.ds(0, size)

        def body(i, total):
            rows = pl.ds(pl.multiple_of(i * ROWS, ROWS), ROWS)
            upper_rows = pl.ds(pl.multiple_of(units + i * ROWS, ROWS), ROWS)
            gate, upper = both[rows, used], both[upper_rows, used]
            read = readout[rows, lanes].astype(F32)
            sigma = jax.nn.sigmoid(gate)
            silu = gate * sigma
            hidden = (silu * upper).astype(BF16).astype(F32)
            grads[rows, lanes] = read * upper * sigma * (1.0 + gate * (1.0 - sigma))
            grads[upper_rows, lanes] = read * silu
            return total + jnp.sum(hidden * read, axis=0, keepdims=True)

        total = lax.fori_loop(0, units // ROWS, body, jnp.zeros((1, size), F32))
        token_score[:, lanes] += total

    def unit_reference(c):
        start, size = CHUNKS[c]
        lanes, used = pl.ds(start, size), pl.ds(128 if c == LAST else 0, size)

        def body(i, total):
            rows = pl.ds(pl.multiple_of(i * ROWS, ROWS), ROWS)
            upper_rows = pl.ds(pl.multiple_of(units + i * ROWS, ROWS), ROWS)
            gate, upper = both[rows, used], both[upper_rows, used]
            read = readout[rows, lanes].astype(F32)
            hidden = (gate * jax.nn.sigmoid(gate) * upper).astype(BF16).astype(F32)
            return total + jnp.sum(hidden * read, axis=0, keepdims=True)

        total = lax.fori_loop(0, units // ROWS, body, jnp.zeros((1, size), F32))
        token_score[:, lanes] -= total

    def policy_units(c):
        return [
            functools.partial(unit_project, policy, gate_rows, c),
            functools.partial(unit_project, policy, up_rows, c),
            functools.partial(unit_policy, c),
        ]

    def reference_units(c):
        return [
            functools.partial(unit_project, outer, gate_rows, c),
            functools.partial(unit_project, outer, up_rows, c),
            functools.partial(unit_reference, c),
        ]

    todo = [unit_mask] + [functools.partial(unit_order, start) for start in range(0, GROUP_TOK, 256)]
    local[0].wait()
    left = {s: PIECES for s in RANK}
    early = {(s, p) for s, p in ORDER[PIECES:] if p < PIECES // 2 and RANK[s] * LEN >= CHUNKS[LAST][0]}
    early |= {(s, p) for s, p in ORDER[PIECES:] if RANK[s] * LEN < CHUNKS[LAST][0]}
    halved = False
    for s, p in ORDER[PIECES:]:
        copies[s, p].wait_recv()
        for piece in CHILDREN.get((s, p), []):
            copies[piece].start()
        early.discard((s, p))
        if not early and not halved:
            for unit in todo + last_halves(0):
                unit()
            todo, halved = [], True
        left[s] -= 1
        if left[s]:
            continue
        rank = RANK[s]
        if rank == 19:
            gate_far.wait_recv()
            gate_pass.start()
        if rank == 33:
            up_far.wait_recv()
            up_pass.start()
        if rank == 37:
            local[5].wait()
            local[6].wait()
            for copy in (gate_near, up_near, gate_pass, up_pass):
                copy.wait_recv()
            todo += reference_units(0) + reference_units(1)
        for c, (start, size) in enumerate(CHUNKS):
            if (rank + 1) * LEN != start + size or c == LAST:
                continue
            todo += policy_units(c)
            if c >= 2:
                todo += reference_units(c)
        if todo and rank >= 7:
            todo.pop(0)()
    for unit in todo + last_halves(1) + [functools.partial(unit_policy, LAST), functools.partial(unit_reference, LAST)]:
        unit()

    belongs = iota((SEQS, GROUP_TOK), 0) == sequence
    partial = jnp.sum(jnp.where(belongs, token_score[...], 0.0), axis=1, keepdims=True)
    partial = column_to_row(partial, SEQS, BLOCK)
    own_score[...] = partial
    offsets = [(d // 4 % 2, d % 4, d // 8) for d in range(1, SEQS)]
    offsets.sort(key=lambda o: -(2 * o[0] + min(o[1], NY - o[1]) + min(o[2], NZ - o[2])))

    def score_copy(slot, n, offset):
        return pltpu.make_async_remote_copy(
            src_ref=own_score, dst_ref=scores.at[slot], send_sem=sum_send.at[n], recv_sem=sum_recv.at[slot],
            device_id=(rep, at(*offset)), device_id_type=MESH,
        )

    score_copies = [score_copy(me, n, offset) for n, offset in enumerate(offsets)]
    for copy in score_copies:
        copy.start()
    scores[me] = partial

    for copy in slab_copies:
        copy.wait_recv()
    local[4].wait()
    local[7].wait()
    STEP = 16

    def pseudo(i, _):
        rows = pl.ds(pl.multiple_of(i * STEP, STEP), STEP)
        for b in range(part // BLOCK):
            lanes = slice(b * BLOCK, (b + 1) * BLOCK)
            own_block = own[rows, lanes].astype(F32)
            total = jnp.zeros((STEP, BLOCK), F32)
            for r in range(4):
                delta = own_block - slabs[r, rows, lanes].astype(F32)
                scale = jnp.max(jnp.abs(delta), axis=1, keepdims=True) + tiny_eps
                scale = scale.astype(BF16).astype(F32)
                total += (delta / scale).astype(BF16).astype(F32) * scale
            average[rows, lanes] = total * 0.25
        return 0

    lax.fori_loop(0, units // STEP, pseudo, 0)

    for piece in ORDER[PIECES:]:
        copies[piece].wait_send()
    for copy in (gate_far, up_far, gate_near, up_near, gate_pass, up_pass, *slab_copies):
        copy.wait_send()
    for n, offset in enumerate(offsets):
        score_copy(at(*offset), n, offset).wait_recv()
    relative_out[...] = jnp.sum(scores[...], axis=0)

    for copy in score_copies:
        copy.wait_send()


def gather_forward(codes, mask, tokens, readout_t, w_gate, w_up, outer_gate, outer_up):
    units, width = w_gate.shape
    part = outer_gate.shape[1]
    vmem_spec = pl.BlockSpec(memory_space=pltpu.VMEM)
    return pl.pallas_call(
        gather_kernel,
        name="gather_forward",
        out_shape=(
            jax.ShapeDtypeStruct((GROUP_TOK, width), BF16),
            jax.ShapeDtypeStruct((2 * units, GROUP_TOK), F32),
            jax.ShapeDtypeStruct((units, part), F32),
            jax.ShapeDtypeStruct((1, BLOCK), F32),
        ),
        in_specs=[pl.BlockSpec(memory_space=pltpu.HBM)] * 8,
        out_specs=(vmem_spec,) * 4,
        scratch_shapes=[
            pltpu.VMEM((1, GROUP_TOK), jnp.int32),
            pltpu.VMEM((1, GROUP_TOK), jnp.int32),
            pltpu.VMEM((2 * units, width), BF16),
            pltpu.VMEM((2 * units, width), BF16),
            pltpu.VMEM((units, part), BF16),
            pltpu.VMEM((4, units, part), BF16),
            pltpu.VMEM((units, GROUP_TOK), BF16),
            pltpu.VMEM((units, GROUP_TOK), BF16),
            pltpu.VMEM((2 * units, 256), F32),
            pltpu.VMEM((1, GROUP_TOK), F32),
            pltpu.VMEM((SEQS, 1, BLOCK), F32),
            pltpu.VMEM((1, BLOCK), F32),
            pltpu.SemaphoreType.DMA((10,)),
            pltpu.SemaphoreType.DMA((SEQS * PIECES,)),
            pltpu.SemaphoreType.DMA((SEQS * PIECES,)),
            pltpu.SemaphoreType.DMA((9,)),
            pltpu.SemaphoreType.DMA((9,)),
            pltpu.SemaphoreType.DMA((SEQS,)),
            pltpu.SemaphoreType.DMA((SEQS,)),
        ],
        compiler_params=pltpu.CompilerParams(
            collective_id=0, has_side_effects=True, vmem_limit_bytes=K1_LIMIT
        ),
    )(*(pltpu.with_memory_space_constraint(a, pltpu.HBM) for a in (
        codes, mask, tokens, readout_t, w_gate, w_up, outer_gate, outer_up
    )))


STEPS = 8


def backward_kernel(
    codes_ref, order_ref, relative_ref, grads, x_all, average, outer, moment,
    loss_out, gate_hbm, up_hbm, new_outer_hbm, new_moment_hbm,
    scaled, products, new_outer, new_moment, state_sem, out_sem,
):
    units = outer.shape[0]
    width = x_all.shape[1]
    block, slab = width // STEPS, outer.shape[1] // STEPS
    pairs = SEQS // 2

    relative = row_to_column(relative_ref[...], SEQS, BLOCK)
    placed = iota((SEQS, SEQS), 0) == order_ref[...]
    by_place = jnp.sum(jnp.where(placed, relative, 0.0), axis=0, keepdims=True)
    place, pair = iota((pairs, SEQS), 1), iota((pairs, SEQS), 0)
    sign = jnp.where(place == 2 * pair, 1.0, jnp.where(place == 2 * pair + 1, -1.0, 0.0))
    margin = dpo_beta * jnp.sum(sign * by_place, axis=1, keepdims=True)
    loss_out[0] = jnp.sum(jax.nn.softplus(-margin)) / pairs
    weight = dpo_beta * jax.nn.sigmoid(-margin) / pairs
    place_coef = jnp.sum(-sign * weight, axis=0, keepdims=True)
    coef = jnp.sum(jnp.where(placed, place_coef, 0.0), axis=1, keepdims=True)
    belongs = iota((SEQS, GROUP_TOK), 0) == sequence_of(codes_ref[...])
    token_grad = jnp.sum(jnp.where(belongs, coef, 0.0), axis=0, keepdims=True)
    scaled[...] = (grads[...] * token_grad).astype(BF16)

    out_copies = []
    for i in range(STEPS):
        cols = pl.ds(i * block, block)
        products[:, cols] = jnp.dot(
            scaled[...], x_all[:, cols], preferred_element_type=F32
        ).astype(BF16)
        lanes = slice(i * slab, (i + 1) * slab)
        fresh = outer_mu * moment[:, lanes] + average[:, lanes]
        new_moment[:, lanes] = fresh
        new_outer[:, lanes] = (
            outer[:, lanes].astype(F32) - outer_rate * (average[:, lanes] + outer_mu * fresh)
        ).astype(BF16)
        out_copies += [
            pltpu.make_async_copy(
                products.at[pl.ds(0, units), cols], gate_hbm.at[0, :, cols], out_sem.at[2 * i]
            ),
            pltpu.make_async_copy(
                products.at[pl.ds(units, units), cols], up_hbm.at[0, :, cols], out_sem.at[2 * i + 1]
            ),
        ]
        out_copies[-2].start()
        out_copies[-1].start()
    out_copies += [
        pltpu.make_async_copy(new_outer, new_outer_hbm, state_sem.at[0]),
        pltpu.make_async_copy(new_moment, new_moment_hbm, state_sem.at[1]),
    ]
    out_copies[-2].start()
    out_copies[-1].start()
    for copy in out_copies:
        copy.wait()


def backward(codes, order, relative, grads, x_all, average, outer_gate, moment):
    units, part = outer_gate.shape
    width = x_all.shape[1]
    any_spec = pl.BlockSpec(memory_space=pl.ANY)
    vmem_spec = pl.BlockSpec(memory_space=pltpu.VMEM)
    return pl.pallas_call(
        backward_kernel,
        name="backward",
        out_shape=(
            jax.ShapeDtypeStruct((1,), F32),
            jax.ShapeDtypeStruct((1, units, width), BF16),
            jax.ShapeDtypeStruct((1, units, width), BF16),
            jax.ShapeDtypeStruct((units, part), BF16),
            jax.ShapeDtypeStruct((units, part), F32),
        ),
        in_specs=[vmem_spec] * 8,
        out_specs=(pl.BlockSpec(memory_space=pltpu.SMEM),) + (any_spec,) * 4,
        scratch_shapes=[
            pltpu.VMEM((2 * units, GROUP_TOK), BF16),
            pltpu.VMEM((2 * units, width), BF16),
            pltpu.VMEM((units, part), BF16),
            pltpu.VMEM((units, part), F32),
            pltpu.SemaphoreType.DMA((2,)),
            pltpu.SemaphoreType.DMA((2 * STEPS,)),
        ],
        compiler_params=pltpu.CompilerParams(vmem_limit_bytes=K2_LIMIT),
    )(codes, order, relative, grads, x_all, average, outer_gate, moment)


def per_device(tokens, readout, resp_mask, order, w_gate, w_up, outer_gate, outer_up, moment):
    codes = jnp.asarray(position_codes())
    x_all, grads, average, relative = gather_forward(
        codes, resp_mask.reshape(1, -1), tokens, readout.T, w_gate[0], w_up[0], outer_gate, outer_up
    )
    return backward(codes, order, relative, grads, x_all, average, outer_gate, moment)


def solution(mesh):
    return jax.shard_map(
        per_device,
        mesh=mesh,
        in_specs=(
            P(("rep", "fsdp"), None),
            P("rep", "fsdp"),
            P("rep"),
            P("rep", None),
            P("rep", "fsdp", None),
            P("rep", "fsdp", None),
            P("fsdp", "rep"),
            P("fsdp", "rep"),
            P("fsdp", "rep"),
        ),
        out_specs=(
            P("rep"),
            P("rep", "fsdp", None),
            P("rep", "fsdp", None),
            P("fsdp", "rep"),
            P("fsdp", "rep"),
        ),
        check_vma=False,
    )
```
